256 devices in a mesh: dp: 8 (over y, core), proto: 32 (over z, x).
Axes of the slice: x: 4, y: 4, z: 8, core: 2. Of those that a mesh axis runs over, the one named last changes fastest.
Arguments:
- teacher_features: bfloat16 [6144, 384], P('dp'), may hold values from -8 to 8
- student_features: bfloat16 [6144, 384], P('dp'), may hold values from -8 to 8
- teacher_weight: bfloat16 [384, 131072], P('dp', 'proto'), may hold values from -1 to 1
- student_weight: bfloat16 [384, 131072], P('dp', 'proto'), may hold values from -1 to 1
Outputs:
- teacher_codes: bfloat16 [6144, 131072], P('dp', 'proto')
- head_loss: float32 [], replicated
- weight_grad: float32 [384, 131072], P('dp', 'proto')
The draws below stay inside these ranges and needn't reach their ends.
All inputs are finite; a program needn't handle non-finite values.
Results may differ from the reference program's by a relative error of at most 0.003.
Values may be sent and summed in bfloat16 or wider, within the bound.
A program may use at most 128 MiB of HBM per device.

```python
import jax
import jax.numpy as jnp
from jax import lax

BOTTLE = 384
PROTOS = 131072
ITERS = 3
CROPS = 6144
N_PROTO = 32


def prototype_table(key, salt_value):
    table_key = jax.random.fold_in(key, salt_value)
    spread = BOTTLE ** (-0.5)
    table_base = jnp.clip(jax.random.normal(table_key, (BOTTLE, PROTOS), jnp.float32), -4.0, 4.0) * spread
    return table_base


def feature_table(key, salt_value, spread):
    feature_key = jax.random.fold_in(key, salt_value + 10)
    features = jnp.clip(jax.random.normal(feature_key, (CROPS, BOTTLE), jnp.float32), -6.0, 6.0) * spread
    return features


def draw_teacher_weight(key, part):
    return prototype_table(key, 1).astype(jnp.bfloat16)


def draw_student_weight(key, part):
    return prototype_table(key, 2).astype(jnp.bfloat16)


def draw_teacher_features(key, part):
    return feature_table(key, 1, 0.25).astype(jnp.bfloat16)


def draw_student_features(key, part):
    return feature_table(key, 2, 0.3).astype(jnp.bfloat16)


def setup_inputs(seed: int = 0) -> dict:
    keys = jax.random.split(jax.random.key(seed), 5)
    teacher_features = draw_teacher_features(jax.random.fold_in(keys[4], 71), 0)
    student_features = draw_student_features(jax.random.fold_in(keys[4], 71), 0)
    teacher_weight = draw_teacher_weight(jax.random.fold_in(keys[4], 71), 0)
    student_weight = draw_student_weight(jax.random.fold_in(keys[4], 71), 0)
    return dict(teacher_features=teacher_features, student_features=student_features, teacher_weight=teacher_weight, student_weight=student_weight)


teacher_temp = 0.07
student_temp = 0.1
norm_eps = 1e-06

def block_logits(features, weight, block_index, block_width):
    weight_piece = lax.dynamic_slice_in_dim(weight, (block_index * block_width).astype(jnp.int32), block_width, 1)
    piece_norm = jnp.sqrt(lax.optimization_barrier(jnp.sum(jnp.square(weight_piece.astype(jnp.float32)), axis=0)) + norm_eps)
    logits = jnp.dot(features, weight_piece, preferred_element_type=jnp.float32) / piece_norm
    return (logits, weight_piece, piece_norm)

def reference(teacher_features, student_features, teacher_weight, student_weight):
    block_width = PROTOS // N_PROTO
    blocks = jnp.arange(N_PROTO, dtype=jnp.int32)

    def block_peaks(block_index):
        teacher_block, _, _ = block_logits(teacher_features, teacher_weight, block_index, block_width)
        student_block, _, _ = block_logits(student_features, student_weight, block_index, block_width)
        return (lax.optimization_barrier(jnp.max(teacher_block, axis=1)), lax.optimization_barrier(jnp.max(student_block, axis=1)))
    teacher_peaks, student_peaks = lax.map(block_peaks, blocks)
    teacher_peak = lax.optimization_barrier(jnp.max(teacher_peaks, axis=0))
    student_peak = lax.optimization_barrier(jnp.max(student_peaks, axis=0))

    def powers_of(block_index):
        teacher_block, _, _ = block_logits(teacher_features, teacher_weight, block_index, block_width)
        return jnp.exp((teacher_block - teacher_peak[:, None]) / teacher_temp)

    def student_part(block_index):
        student_block, _, _ = block_logits(student_features, student_weight, block_index, block_width)
        shifted = (student_block - student_peak[:, None]) / student_temp
        return lax.optimization_barrier(jnp.sum(jnp.exp(shifted), axis=1))
    student_total = lax.optimization_barrier(jnp.sum(lax.map(student_part, blocks), axis=0))
    crop_scale = jnp.ones((CROPS,), jnp.float32)
    proto_scale = jnp.ones((N_PROTO, block_width), jnp.float32)
    for sweep_index in range(ITERS):

        def column_part(block_index, scale_now=crop_scale):
            return jnp.dot(scale_now, powers_of(block_index), precision=lax.Precision.HIGHEST)
        proto_mass = lax.map(column_part, blocks)
        proto_scale = 1.0 / (PROTOS * proto_mass)

        def row_part(paired):
            block_index, scale_block = paired
            return jnp.dot(powers_of(block_index), scale_block, precision=lax.Precision.HIGHEST)
        crop_mass = lax.optimization_barrier(jnp.sum(lax.map(row_part, (blocks, proto_scale)), axis=0))
        crop_scale = 1.0 / (CROPS * crop_mass)

    def finish(paired):
        block_index, scale_block = paired
        powers = powers_of(block_index)
        assign = powers * scale_block[None, :] * crop_scale[:, None] * CROPS
        student_block, weight_piece, student_norm = block_logits(student_features, student_weight, block_index, block_width)
        shifted = (student_block - student_peak[:, None]) / student_temp
        log_prob = shifted - jnp.log(student_total)[:, None]
        loss_part = -jnp.sum(assign * log_prob)
        signal = ((jnp.exp(log_prob) - assign) / student_temp).astype(jnp.bfloat16)
        direct = lax.dot_general(student_features, signal, (((0,), (0,)), ((), ())), preferred_element_type=jnp.float32)
        pressure = lax.optimization_barrier(jnp.sum(signal.astype(jnp.float32) * student_block, axis=0))
        grad_block = (direct - weight_piece.astype(jnp.float32) / student_norm * pressure[None, :]) / student_norm
        return (assign.astype(jnp.bfloat16), loss_part, grad_block)
    code_blocks, loss_parts, grad_blocks = lax.map(finish, (blocks, proto_scale))
    teacher_codes = jnp.transpose(code_blocks, (1, 0, 2)).reshape(CROPS, PROTOS)
    weight_grad = jnp.transpose(grad_blocks, (1, 0, 2)).reshape(BOTTLE, PROTOS)
    head_loss = jnp.sum(loss_parts) / CROPS
    return (teacher_codes, head_loss, weight_grad)
```

```python
import functools

import jax
import jax.numpy as jnp
from jax import lax
from jax.experimental import pallas as pl
from jax.experimental.pallas import tpu as pltpu
from jax.sharding import PartitionSpec as P

ITERS = 3


teacher_temp = 0.07
student_temp = 0.1
norm_eps = 1e-06
MESH = pl.DeviceIdType.MESH


def exchange_kernel(axis, n, op, x_ref, o_ref, buf, send_sem, recv_sem):
    me = lax.axis_index(axis)
    barrier = pltpu.get_barrier_semaphore()

    @pl.loop(1, n)
    def _(o):
        pl.semaphore_signal(barrier, inc=1, device_id={axis: lax.rem(me + o, n)}, device_id_type=MESH)

    pl.semaphore_wait(barrier, n - 1)

    @pl.loop(1, n)
    def _(o):
        pltpu.make_async_remote_copy(
            src_ref=x_ref,
            dst_ref=buf.at[o - 1],
            send_sem=send_sem,
            recv_sem=recv_sem,
            device_id={axis: lax.rem(me + o, n)},
            device_id_type=MESH,
        ).start()

    whole = pltpu.make_async_remote_copy(
        src_ref=buf, dst_ref=buf, send_sem=send_sem, recv_sem=recv_sem,
        device_id={axis: lax.rem(me + 1, n)}, device_id_type=MESH,
    )
    whole.wait_recv()
    total = x_ref[...]
    for o in range(1, n):
        total = op(total, buf[o - 1])
    o_ref[...] = total
    whole.wait_send()


def exchange(x, axis, op, collective_id):
    n = lax.axis_size(axis)
    rows = x.shape[0]
    return pl.pallas_call(
        functools.partial(exchange_kernel, axis, n, op),
        out_shape=jax.ShapeDtypeStruct(x.shape, jnp.float32),
        in_specs=[pl.BlockSpec(memory_space=pltpu.VMEM)],
        out_specs=pl.BlockSpec(memory_space=pltpu.VMEM),
        scratch_shapes=[
            pltpu.VMEM((n - 1, rows, 128), jnp.float32),
            pltpu.SemaphoreType.DMA,
            pltpu.SemaphoreType.DMA,
        ],
        compiler_params=pltpu.CompilerParams(collective_id=collective_id, has_side_effects=True),
    )(x)


def column_norm(weight_rows):
    return jnp.sqrt(jnp.sum(jnp.square(weight_rows.astype(jnp.float32)), axis=0) + norm_eps)


def pack(x):
    return jnp.pad(x.reshape(6, 128), ((0, 2), (0, 0)))


def body(teacher_features, student_features, teacher_weight, student_weight):
    local_crops = teacher_features.shape[0]
    total_crops = local_crops * lax.axis_size("dp")
    total_protos = teacher_weight.shape[1] * lax.axis_size("proto")
    teacher_full, student_full = (
        lax.all_gather(teacher_weight, "dp", axis=0, tiled=True),
        lax.all_gather(student_weight, "dp", axis=0, tiled=True),
    )
    teacher_norm = column_norm(teacher_full)
    student_norm = column_norm(student_full)
    teacher_logits = (
        jnp.dot(teacher_features, teacher_full, preferred_element_type=jnp.float32) / teacher_norm
    )
    student_logits = (
        jnp.dot(student_features, student_full, preferred_element_type=jnp.float32) / student_norm
    )
    peaks = exchange(
        jnp.concatenate([pack(jnp.max(teacher_logits, axis=1)), pack(jnp.max(student_logits, axis=1))]),
        "proto", jnp.maximum, 0,
    )
    teacher_peak = peaks[:6].reshape(-1)
    student_peak = peaks[8:14].reshape(-1)
    powers = jnp.exp((teacher_logits - teacher_peak[:, None]) / teacher_temp)
    shifted = (student_logits - student_peak[:, None]) / student_temp
    student_local = jnp.sum(jnp.exp(shifted), axis=1)
    crop_scale = jnp.ones((local_crops,), jnp.float32)
    for sweep_index in range(ITERS):
        proto_mass = exchange(
            jnp.sum(crop_scale[:, None] * powers, axis=0).reshape(32, 128), "dp", jnp.add, 1
        ).reshape(-1)
        proto_scale = 1.0 / (total_protos * proto_mass)
        crop_local = jnp.sum(powers * proto_scale, axis=1)
        sums = exchange(jnp.concatenate([pack(crop_local), pack(student_local)]), "proto", jnp.add, 2)
        crop_mass = sums[:6].reshape(-1)
        student_total = sums[8:14].reshape(-1)
        crop_scale = 1.0 / (total_crops * crop_mass)
    assign = powers * proto_scale[None, :] * crop_scale[:, None] * total_crops
    teacher_codes = assign.astype(jnp.bfloat16)
    log_prob = shifted - jnp.log(student_total)[:, None]
    loss_local = -jnp.sum(assign * log_prob)
    signal = ((jnp.exp(log_prob) - assign) / student_temp).astype(jnp.bfloat16)
    head_loss = lax.psum(loss_local, ("dp", "proto")) / total_crops
    own_weight = student_weight.astype(jnp.float32) / student_norm
    own_grad = lax.psum_scatter(
        lax.dot_general(
            student_features, signal, (((0,), (0,)), ((), ())), preferred_element_type=jnp.float32
        ),
        "dp",
        scatter_dimension=0,
        tiled=True,
    )
    pressure = exchange(jnp.sum(own_grad * own_weight, axis=0).reshape(32, 128), "dp", jnp.add, 1).reshape(-1)
    weight_grad = (own_grad - own_weight * pressure[None, :]) / student_norm
    return (teacher_codes, head_loss, weight_grad)


def solution(mesh):
    return jax.shard_map(
        body,
        mesh=mesh,
        in_specs=(P("dp", None), P("dp", None), P("dp", "proto"), P("dp", "proto")),
        out_specs=(P("dp", "proto"), P(), P("dp", "proto")),
        check_vma=False,
    )
```

```python
import math

import jax
import jax.numpy as jnp
from jax import lax
from jax.experimental import pallas as pl
from jax.experimental.pallas import tpu as pltpu
from jax.sharding import PartitionSpec as P

ITERS = 3
teacher_temp = 0.07
student_temp = 0.1
norm_eps = 1e-06
MESH = pl.DeviceIdType.MESH
LOG2E = math.log2(math.e)
LN2 = math.log(2.0)
F32 = jnp.float32
BF16 = jnp.bfloat16

NY, NX, NZ = 4, 4, 8
NDP = 2 * NY
CROPS = 768
PROTOS = 4096
BOTTLE = 384
SLAB = BOTTLE // NDP
LANES = 128
GROUPS = PROTOS // LANES
CBLK = CROPS // LANES
NCHUNK = 4
CHUNK = PROTOS // NCHUNK
FCHUNK = 512
NF = PROTOS // FCHUNK
TOTAL_CROPS = CROPS * NDP
TOTAL_PROTOS = PROTOS * NX * NZ


def remote(src, dst, send, recv, **device):
    return pltpu.make_async_remote_copy(
        src_ref=src, dst_ref=dst, send_sem=send, recv_sem=recv, device_id=device, device_id_type=MESH
    )


def head_kernel(
    tf, sf, tw, sw,
    codes, loss_out, grad,
    TW, SW, Z, S, sfT, part, zcol, ccol, lcol, crow, prow, pstmp, isn,
    stage, sig, ownf, sendsib, recvsib, sendy, recvy,
    dbuf, dbuf4, xbuf, zbuf, xbuf3, zbuf3,
    local_sem, code_sem, t_send, t_recv, s_send, s_recv,
    d_send, d_recv, x_send, x_recv, z_send, z_recv, sib_send, sib_recv, y_send, y_recv,
):
    j = lax.axis_index("dp")
    p = lax.axis_index("proto")
    y, core = lax.div(j, 2), lax.rem(j, 2)
    z, x = lax.div(p, NX), lax.rem(p, NX)
    sib = 2 * y + (1 - core)

    def ypeer(o):
        return 2 * lax.rem(y + o, NY) + core

    def xpeer(o):
        return z * NX + lax.rem(x + o, NX)

    def zpeer(o):
        return lax.rem(z + o, NZ) * NX + x

    barrier = pltpu.get_barrier_semaphore()

    @pl.loop(1, NDP)
    def _(o):
        pl.semaphore_signal(barrier, inc=1, device_id={"dp": lax.rem(j + o, NDP)}, device_id_type=MESH)

    @pl.loop(1, NX)
    def _(o):
        pl.semaphore_signal(barrier, inc=1, device_id={"proto": xpeer(o)}, device_id_type=MESH)

    @pl.loop(1, NZ)
    def _(o):
        pl.semaphore_signal(barrier, inc=1, device_id={"proto": zpeer(o)}, device_id_type=MESH)

    pl.semaphore_wait(barrier, (NDP - 1) + (NX - 1) + (NZ - 1))

    def rows_of(index):
        return pl.ds(pl.multiple_of(index * SLAB, 16), SLAB)

    def cols_of(q):
        return pl.ds(pl.multiple_of(q * CHUNK, CHUNK), CHUNK)

    @pl.loop(0, NCHUNK)
    def _(q):
        src = tw.at[:, cols_of(q)]
        dst = TW.at[rows_of(j), cols_of(q)]
        remote(src, dst, t_send, t_recv.at[q, 0], dp=ypeer(1)).start()
        remote(src, dst, t_send, t_recv.at[q, 1], dp=ypeer(3)).start()
        remote(src, dst, t_send, t_recv.at[q, 4], dp=sib).start()

    own_t = pltpu.make_async_copy(tw, TW.at[rows_of(j)], local_sem.at[0])
    own_s = pltpu.make_async_copy(sw, SW.at[rows_of(j)], local_sem.at[1])
    own_t.start()
    own_s.start()

    for half in range(2):
        for slab in range(NY):
            index = 2 * slab + half
            block = sf[:, index * SLAB:(index + 1) * SLAB].astype(F32)
            sfT[half, slab * SLAB:(slab + 1) * SLAB, :] = jnp.transpose(block).astype(BF16)

    def t_wait(q, kind, index, half=None):
        if half is None:
            region = TW.at[rows_of(index), cols_of(q)]
        else:
            start = pl.multiple_of(q * CHUNK + half * (CHUNK // 2), CHUNK // 2)
            region = TW.at[rows_of(index), pl.ds(start, CHUNK // 2)]
        remote(region, region, t_send, t_recv.at[q, kind], dp=sib).wait_recv()
        return region

    left, right, far = ypeer(3), ypeer(1), ypeer(2)

    @pl.loop(0, NCHUNK)
    def _(q):
        region = t_wait(q, 0, left)
        a = TW.at[rows_of(left), pl.ds(pl.multiple_of(q * CHUNK, CHUNK), CHUNK // 2)]
        remote(a, a, t_send, t_recv.at[q, 2], dp=right).start()
        remote(region, region, t_send, t_recv.at[q, 5], dp=sib).start()
        region = t_wait(q, 1, right)
        b = TW.at[rows_of(right), pl.ds(pl.multiple_of(q * CHUNK + CHUNK // 2, CHUNK // 2), CHUNK // 2)]
        remote(b, b, t_send, t_recv.at[q, 3], dp=left).start()
        remote(region, region, t_send, t_recv.at[q, 6], dp=sib).start()

    mine = SW.at[rows_of(j)]
    for o in (1, 3, 2):
        remote(sw, mine, s_send, s_recv.at[o - 1], dp=ypeer(o)).start()
    remote(sw, mine, s_send, s_recv.at[3], dp=sib).start()
    own_t.wait()
    own_s.wait()

    def logits_chunk(q, feat, W, OUT, constant, keep):
        cols = cols_of(q)

        def square(r, acc):
            w = W[pl.ds(pl.multiple_of(r * 16, 16), 16), cols].astype(F32)
            w = w * w
            return acc + (w[:8] + w[8:])

        acc = lax.fori_loop(0, BOTTLE // 16, square, jnp.zeros((8, CHUNK), F32), unroll=4)
        inverse = 1.0 / jnp.sqrt(jnp.sum(acc, axis=0, keepdims=True) + norm_eps)
        if keep is not None:
            keep[:, cols] = jnp.broadcast_to(inverse, (8, CHUNK))
        crow[...] = jnp.broadcast_to(inverse * constant, (8, CHUNK))

        @pl.loop(0, CHUNK // 256)
        def _(b):
            inner = pl.ds(pl.multiple_of(q * CHUNK + b * 256, 256), 256)
            value = jnp.dot(feat[...], W[:, inner], preferred_element_type=F32)
            value = value * crow[0:1, pl.ds(pl.multiple_of(b * 256, 256), 256)]
            OUT[:, inner] = value
            part[...] = jnp.maximum(part[...], jnp.maximum(value[:, :128], value[:, 128:]))

    part[...] = jnp.full((CROPS, LANES), -jnp.inf, F32)

    @pl.loop(0, NCHUNK)
    def _(q):
        t_wait(q, 2, far, 0)
        t_wait(q, 3, far, 1)
        region = TW.at[rows_of(far), cols_of(q)]
        remote(region, region, t_send, t_recv.at[q, 7], dp=sib).start()

    @pl.loop(0, NCHUNK)
    def _(q):
        t_wait(q, 4, sib)
        for kind, o in ((5, 3), (6, 1), (7, 2)):
            t_wait(q, kind, 2 * lax.rem(y + o, NY) + (1 - core))
        logits_chunk(q, tf, TW, Z, LOG2E / teacher_temp, None)

    def start(axis, buf, me, n, peer, send, recv):
        @pl.loop(1, n)
        def _(o):
            slot = buf.at[me]
            remote(slot, slot, send, recv, **{axis: peer(o)}).start()

    def finish(axis, buf, n, peer, send, recv):
        region = buf.at[pl.ds(0, n - 1)]
        remote(region, region, send, recv, **{axis: peer(1)}).wait_recv()

    def done_sending(axis, buf, n, peer, send, recv):
        region = buf.at[pl.ds(0, n - 1)]
        remote(region, region, send, recv, **{axis: peer(1)}).wait_send()

    def dpeer(o):
        return lax.rem(j + o, NDP)

    sent = []

    def over_dp(i, buf):
        args = ("dp", buf, NDP, dpeer, d_send.at[i], d_recv.at[i])
        sent.append(args)
        start("dp", buf, j, NDP, dpeer, d_send.at[i], d_recv.at[i])
        return lambda: finish(*args)

    def over_x(i, buf):
        args = ("proto", buf, NX, xpeer, x_send.at[i], x_recv.at[i])
        sent.append(args)
        start("proto", buf, x, NX, xpeer, x_send.at[i], x_recv.at[i])
        return lambda: finish(*args)

    def over_z(i, buf):
        args = ("proto", buf, NZ, zpeer, z_send.at[i], z_recv.at[i])
        sent.append(args)
        start("proto", buf, z, NZ, zpeer, z_send.at[i], z_recv.at[i])
        return lambda: finish(*args)

    def combine(buf, n, op):
        total = buf[0]
        for k in range(1, n):
            total = op(total, buf[k])
        return total

    def lane_reduce(reduce):
        rows = []
        for i in range(CBLK):
            rows.append(reduce(jnp.transpose(part[i * LANES:(i + 1) * LANES, :]), axis=0, keepdims=True))
        rows.append(jnp.zeros((8 - CBLK, LANES), F32))
        return jnp.concatenate(rows, axis=0)

    def to_columns(value, out):
        for i in range(CBLK):
            out[i * LANES:(i + 1) * LANES, :] = jnp.transpose(jnp.broadcast_to(value[i:i + 1, :], (LANES, LANES)))

    def exp_rows(first, last):
        @pl.loop(first // 8, last // 8)
        def _(r):
            rows = pl.ds(pl.multiple_of(r * 8, 8), 8)
            peak = zcol[rows, :]
            for g in range(GROUPS):
                lanes = pl.ds(g * LANES, LANES)
                Z[rows, lanes] = jnp.exp2(Z[rows, lanes] - peak)

    def proto_pass(out):
        for seg in range(NCHUNK):
            n = CHUNK // LANES

            def step(r, acc):
                rows = pl.ds(pl.multiple_of(r * 8, 8), 8)
                c = ccol[rows, :]
                return tuple(
                    acc[g] + Z[rows, pl.ds(seg * CHUNK + g * LANES, LANES)] * c for g in range(n)
                )

            acc = lax.fori_loop(0, CROPS // 8, step, tuple(jnp.zeros((8, LANES), F32) for _ in range(n)), unroll=8)
            for g in range(n):
                out[pl.ds(seg * n + g, 1), :] = jnp.sum(acc[g], axis=0, keepdims=True)

    def crop_pass():
        @pl.loop(0, CROPS // 32)
        def _(r):
            acc = [jnp.zeros((8, LANES), F32) for _ in range(4)]
            for g in range(GROUPS):
                scale = prow[:, g * LANES:(g + 1) * LANES]
                for k in range(4):
                    rows = pl.ds(pl.multiple_of(r * 32 + k * 8, 8), 8)
                    acc[k] = acc[k] + Z[rows, pl.ds(g * LANES, LANES)] * scale
            for k in range(4):
                part[pl.ds(pl.multiple_of(r * 32 + k * 8, 8), 8), :] = acc[k]

    def student_relay():
        for k, o in ((0, 3), (2, 1), (1, 2)):
            region = SW.at[rows_of(ypeer(o))]
            remote(region, region, s_send, s_recv.at[k], dp=sib).wait_recv()
            remote(region, region, s_send, s_recv.at[4 + k], dp=sib).start()

    def student_arrived():
        region = SW.at[rows_of(sib)]
        remote(region, region, s_send, s_recv.at[3], dp=sib).wait_recv()
        for k, o in ((0, 3), (2, 1), (1, 2)):
            region = SW.at[rows_of(2 * lax.rem(y + o, NY) + (1 - core))]
            remote(region, region, s_send, s_recv.at[4 + k], dp=sib).wait_recv()

    def student_chunk(q):
        logits_chunk(q, sf, SW, S, LOG2E / student_temp, isn)

    def student_sums():
        peak = lane_reduce(jnp.max)
        to_columns(peak, lcol)

        @pl.loop(0, CROPS // 8)
        def _(r):
            rows = pl.ds(pl.multiple_of(r * 8, 8), 8)
            top = lcol[rows, :]
            acc = [jnp.zeros((8, LANES), F32) for _ in range(4)]
            for g in range(GROUPS):
                acc[g % 4] = acc[g % 4] + jnp.exp2(S[rows, pl.ds(g * LANES, LANES)] - top)
            part[rows, :] = (acc[0] + acc[1]) + (acc[2] + acc[3])
        return peak, lane_reduce(jnp.sum)

    own_peak = lane_reduce(jnp.max)
    xbuf[0, x] = own_peak
    wait = over_x(0, xbuf.at[0])
    to_columns(own_peak, zcol)
    exp_rows(0, CROPS // 2)
    wait()
    zbuf[0, z] = combine(xbuf.at[0], NX, jnp.maximum)
    wait = over_z(0, zbuf.at[0])
    exp_rows(CROPS // 2, CROPS)
    wait()
    peak = combine(zbuf.at[0], NZ, jnp.maximum)
    adjust = jnp.exp2(own_peak - peak)
    to_columns(adjust, ccol)

    for it in range(ITERS):
        proto_pass(dbuf.at[it, j])
        wait = over_dp(it, dbuf.at[it])
        if it == 1:
            student_arrived()
            part[...] = jnp.full((CROPS, LANES), -jnp.inf, F32)
            student_chunk(0)
            student_chunk(1)
            student_chunk(2)
            student_chunk(3)
        if it == 2:
            s_peak, s_sum = student_sums()
            xbuf3[x, 8:16] = s_peak
            xbuf3[x, 16:24] = s_sum
        wait()
        pstmp[...] = 1.0 / (TOTAL_PROTOS * combine(dbuf.at[it], NDP, jnp.add))
        for g in range(GROUPS):
            prow[:, g * LANES:(g + 1) * LANES] = jnp.broadcast_to(pstmp[g:g + 1, :], (8, LANES))
        if it == 1:
            zcol[...] = part[...]
        crop_pass()
        crop_local = lane_reduce(jnp.sum) * adjust
        if it == 1:
            part[...] = zcol[...]
        if it < 2:
            xbuf[1 + it, x] = crop_local
            wait = over_x(1 + it, xbuf.at[1 + it])
            if it == 0:
                student_relay()
            wait()
            zbuf[1 + it, z] = combine(xbuf.at[1 + it], NX, jnp.add)
            wait = over_z(1 + it, zbuf.at[1 + it])
            wait()
            crop_mass = combine(zbuf.at[1 + it], NZ, jnp.add)
        else:
            def merge(a, b):
                top = jnp.maximum(a[8:16], b[8:16])
                total = a[16:24] * jnp.exp2(a[8:16] - top) + b[16:24] * jnp.exp2(b[8:16] - top)
                return jnp.concatenate([a[0:8] + b[0:8], top, total], axis=0)

            xbuf3[x, 0:8] = crop_local
            wait = over_x(3, xbuf3)
            wait()
            zbuf3[z] = combine(xbuf3, NX, merge)
            wait = over_z(3, zbuf3)
            wait()
            merged = combine(zbuf3, NZ, merge)
            crop_mass = merged[0:8]
            lse = merged[8:16] + jnp.log2(merged[16:24])
        crop_scale = 1.0 / (TOTAL_CROPS * crop_mass)
        if it < 2:
            to_columns(crop_scale * adjust, ccol)
        else:
            to_columns(crop_scale * adjust * TOTAL_CROPS, ccol)
            to_columns(lse, lcol)

    def fcols(f):
        return pl.ds(pl.multiple_of(f * FCHUNK, FCHUNK), FCHUNK)

    def code_copy(f, slot):
        return pltpu.make_async_copy(stage.at[slot], codes.at[:, fcols(f)], code_sem.at[slot])

    def sib_copy(f):
        return remote(sendsib.at[:, :, fcols(f)], recvsib.at[:, :, fcols(f)], sib_send, sib_recv.at[f], dp=sib)

    def forward(f):
        sib_copy(f).wait_recv()
        for o in range(1, NY):
            to = lax.rem(y + o, NY)
            total = ownf[to, :, fcols(f)] + recvsib[to, :, fcols(f)].astype(F32)
            sendy[o - 1, :, fcols(f)] = total.astype(BF16)
            remote(
                sendy.at[o - 1, :, fcols(f)], recvy.at[o - 1, :, fcols(f)],
                y_send, y_recv.at[o - 1], dp=ypeer(o),
            ).start()

    @pl.loop(0, NF, init_carry=jnp.zeros((16, FCHUNK), F32))
    def loss_acc(f, loss_acc):
        slot = lax.rem(f, 2)

        @pl.when(f >= 2)
        def _():
            code_copy(f - 2, slot).wait()

        scale = jnp.broadcast_to(prow[0:1, fcols(f)], (16, FCHUNK))
        n = FCHUNK // LANES

        def step(r, carry):
            loss, pressure = carry
            rows = pl.ds(pl.multiple_of(r * 16, 16), 16)
            c = jnp.concatenate([ccol[rows, :]] * n, axis=1)
            l = jnp.concatenate([lcol[rows, :]] * n, axis=1)
            assign = Z[rows, fcols(f)] * scale * c
            stage[slot, rows, :] = assign.astype(BF16)
            s = S[rows, fcols(f)]
            logp = s - l
            signal = ((jnp.exp2(logp) - assign) * (1.0 / student_temp)).astype(BF16)
            sig[rows, :] = signal
            return loss + assign * logp, pressure + signal.astype(F32) * s

        loss_acc, pressure = lax.fori_loop(
            0, CROPS // 16, step, (loss_acc, jnp.zeros((16, FCHUNK), F32)), unroll=2
        )
        code_copy(f, slot).start()
        pressure = jnp.sum(pressure, axis=0, keepdims=True) * (LN2 * student_temp)
        for g in range(n):
            dbuf4[j, pl.ds(f * n + g, 1), :] = pressure[:, g * LANES:(g + 1) * LANES]
        other = jnp.dot(sfT[1 - core], sig[...], preferred_element_type=F32)
        sendsib[:, :, fcols(f)] = other.astype(BF16).reshape(NY, SLAB, FCHUNK)
        sib_copy(f).start()
        own = jnp.dot(sfT[core], sig[...], preferred_element_type=F32)
        ownf[:, :, fcols(f)] = own.reshape(NY, SLAB, FCHUNK)

        @pl.when(f >= 1)
        def _():
            forward(f - 1)
        return loss_acc

    forward(NF - 1)

    folded = loss_acc[0:8] + loss_acc[8:16]
    folded = (folded[:, 0:128] + folded[:, 128:256]) + (folded[:, 256:384] + folded[:, 384:512])
    dbuf4[j, GROUPS:GROUPS + 8] = folded
    wait = over_dp(3, dbuf4)
    wait()
    total = combine(dbuf4, NDP, jnp.add)
    xbuf[3, x] = total[GROUPS:]
    wait = over_x(4, xbuf.at[3])
    pstmp[...] = total[:GROUPS]
    wait()
    zbuf[3, z] = combine(xbuf.at[3], NX, jnp.add)
    wait = over_z(4, zbuf.at[3])
    wait()
    loss = combine(zbuf.at[3], NZ, jnp.add)
    loss = jnp.sum(jnp.sum(loss, axis=1, keepdims=True), axis=0, keepdims=True)
    loss_out[...] = jnp.broadcast_to(loss * (-LN2 / TOTAL_CROPS), (8, LANES))

    for o in range(1, NY):
        remote(sendy.at[o - 1], recvy.at[o - 1], y_send, y_recv.at[o - 1], dp=ypeer(o)).wait_recv()

    for f in range(NF):
        cols = slice(f * FCHUNK, (f + 1) * FCHUNK)
        pressure = jnp.concatenate(
            [pstmp[f * 4 + g:f * 4 + g + 1, :] for g in range(FCHUNK // LANES)], axis=1
        )
        inverse = isn[0:1, cols]
        direct = ownf[y, :, cols] + recvsib[y, :, cols].astype(F32)
        for o in range(NY - 1):
            direct = direct + recvy[o, :, cols].astype(F32)
        weight = sw_rows(SW, j, cols).astype(F32)
        grad[:, cols] = (direct - weight * (inverse * pressure)) * inverse

    code_copy(NF - 2, 0).wait()
    code_copy(NF - 1, 1).wait()
    for args in sent:
        done_sending(*args)
    region = TW.at[pl.ds(0, 7 * SLAB)]
    remote(region, region, t_send, t_recv.at[0, 0], dp=sib).wait_send()
    region = SW.at[pl.ds(0, 7 * SLAB)]
    remote(region, region, s_send, s_recv.at[0], dp=sib).wait_send()
    remote(sendsib, recvsib, sib_send, sib_recv.at[0], dp=sib).wait_send()
    remote(sendy, recvy, y_send, y_recv.at[0], dp=ypeer(1)).wait_send()


def sw_rows(SW, j, cols):
    return SW[pl.ds(pl.multiple_of(j * SLAB, 16), SLAB), cols]


def body(teacher_features, student_features, teacher_weight, student_weight):
    vmem = pl.BlockSpec(memory_space=pltpu.VMEM)
    hbm = pl.BlockSpec(memory_space=pl.ANY)
    dma = pltpu.SemaphoreType.DMA
    codes, loss, grad = pl.pallas_call(
        head_kernel,
        out_shape=(
            jax.ShapeDtypeStruct((CROPS, PROTOS), BF16),
            jax.ShapeDtypeStruct((8, LANES), F32),
            jax.ShapeDtypeStruct((SLAB, PROTOS), F32),
        ),
        in_specs=[vmem, vmem, hbm, hbm],
        out_specs=(hbm, vmem, vmem),
        scratch_shapes=[
            pltpu.VMEM((BOTTLE, PROTOS), BF16),
            pltpu.VMEM((BOTTLE, PROTOS), BF16),
            pltpu.VMEM((CROPS, PROTOS), F32),
            pltpu.VMEM((CROPS, PROTOS), F32),
            pltpu.VMEM((2, BOTTLE // 2, CROPS), BF16),
            pltpu.VMEM((CROPS, LANES), F32),
            pltpu.VMEM((CROPS, LANES), F32),
            pltpu.VMEM((CROPS, LANES), F32),
            pltpu.VMEM((CROPS, LANES), F32),
            pltpu.VMEM((8, CHUNK), F32),
            pltpu.VMEM((8, PROTOS), F32),
            pltpu.VMEM((GROUPS, LANES), F32),
            pltpu.VMEM((8, PROTOS), F32),
            pltpu.VMEM((2, CROPS, FCHUNK), BF16),
            pltpu.VMEM((CROPS, FCHUNK), BF16),
            pltpu.VMEM((NY, SLAB, PROTOS), F32),
            pltpu.VMEM((NY, SLAB, PROTOS), BF16),
            pltpu.VMEM((NY, SLAB, PROTOS), BF16),
            pltpu.VMEM((NY - 1, SLAB, PROTOS), BF16),
            pltpu.VMEM((NY - 1, SLAB, PROTOS), BF16),
            pltpu.VMEM((ITERS, NDP, GROUPS, LANES), F32),
            pltpu.VMEM((NDP, GROUPS + 8, LANES), F32),
            pltpu.VMEM((4, NX, 8, LANES), F32),
            pltpu.VMEM((4, NZ, 8, LANES), F32),
            pltpu.VMEM((NX, 24, LANES), F32),
            pltpu.VMEM((NZ, 24, LANES), F32),
            dma((2,)), dma((2,)), dma, dma((NCHUNK, 8)), dma, dma((7,)),
            dma((4,)), dma((4,)), dma((5,)), dma((5,)), dma((5,)), dma((5,)),
            dma, dma((NF,)), dma, dma((NY - 1,)),
        ],
        compiler_params=pltpu.CompilerParams(
            collective_id=0, has_side_effects=True, vmem_limit_bytes=60 * 1024 * 1024
        ),
    )(teacher_features, student_features, teacher_weight, student_weight)
    return codes, loss[0, 0], grad


def solution(mesh):
    return jax.shard_map(
        body,
        mesh=mesh,
        in_specs=(P("dp", None), P("dp", None), P("dp", "proto"), P("dp", "proto")),
        out_specs=(P("dp", "proto"), P(), P("dp", "proto")),
        check_vma=False,
    )
```

```python
import math

import jax
import jax.numpy as jnp
from jax import lax
from jax.experimental import pallas as pl
from jax.experimental.pallas import tpu as pltpu
from jax.sharding import PartitionSpec as P

ITERS = 3
teacher_temp = 0.07
student_temp = 0.1
norm_eps = 1e-06
MESH = pl.DeviceIdType.MESH
LOG2E = math.log2(math.e)
LN2 = math.log(2.0)
F32 = jnp.float32
BF16 = jnp.bfloat16

NY, NX, NZ = 4, 4, 8
NDP = 2 * NY
NPR = NX * NZ
CROPS = 768
PROTOS = 4096
BOTTLE = 384
SLAB = BOTTLE // NDP
LANES = 128
GROUPS = PROTOS // LANES
CBLK = CROPS // LANES
NCHUNK = 4
CHUNK = PROTOS // NCHUNK
FCHUNK = 512
NF = PROTOS // FCHUNK
NWRITE = 4
TOTAL_CROPS = CROPS * NDP
TOTAL_PROTOS = PROTOS * NPR


def remote(src, dst, send, recv, **device):
    return pltpu.make_async_remote_copy(
        src_ref=src, dst_ref=dst, send_sem=send, recv_sem=recv, device_id=device, device_id_type=MESH
    )


def head_kernel(
    tf, sf, tw, sw,
    codes, loss_out, grad,
    TW, SW, Z, S, sfT, part, spart, zcol, ccol, lcol, crow, prow, pstmp, isn,
    sig, ownf, sendsib, recvsib, sendy, recvy,
    dbuf, dbuf4, pbuf0, pbuf1, pbuf2, pbuf3,
    local_sem, t_send, t_recv, s_send, s_recv,
    d_send, d_recv, p_send, p_recv, sib_send, sib_recv, y_send, y_recv,
):
    j = lax.axis_index("dp")
    p = lax.axis_index("proto")
    y, core = lax.div(j, 2), lax.rem(j, 2)
    z, x = lax.div(p, NX), lax.rem(p, NX)
    sib = 2 * y + (1 - core)

    def ypeer(o):
        return 2 * lax.rem(y + o, NY) + core

    def swing(i, n):
        return n // 2 + lax.div(i + 1, 2) * (1 - 2 * lax.rem(i, 2))

    def dpeer(i):
        return 2 * lax.rem(y + swing(lax.div(i, 2), NY), NY) + lax.rem(core + 1 + i, 2)

    def ppeer(i):
        return lax.rem(z + swing(lax.div(i, NX), NZ), NZ) * NX + lax.rem(x + 1 + i, NX)

    barrier = pltpu.get_barrier_semaphore()

    @pl.loop(0, NPR - 1)
    def _(i):
        pl.semaphore_signal(barrier, inc=1, device_id={"proto": ppeer(i)}, device_id_type=MESH)

    @pl.loop(0, NDP - 1)
    def _(i):
        pl.semaphore_signal(barrier, inc=1, device_id={"dp": dpeer(i)}, device_id_type=MESH)

    pl.semaphore_wait(barrier, (NDP - 1) + (NPR - 1))

    def rows_of(index):
        return pl.ds(pl.multiple_of(index * SLAB, 16), SLAB)

    def cols_of(q):
        return pl.ds(pl.multiple_of(q * CHUNK, CHUNK), CHUNK)

    @pl.loop(0, NCHUNK)
    def _(q):
        src = tw.at[:, cols_of(q)]
        dst = TW.at[rows_of(j), cols_of(q)]
        remote(src, dst, t_send, t_recv.at[q, 0], dp=ypeer(1)).start()
        remote(src, dst, t_send, t_recv.at[q, 1], dp=ypeer(3)).start()
        remote(src, dst, t_send, t_recv.at[q, 4], dp=sib).start()

    own_t = pltpu.make_async_copy(tw, TW.at[rows_of(j)], local_sem.at[0])
    own_s = pltpu.make_async_copy(sw, SW.at[rows_of(j)], local_sem.at[1])
    own_t.start()
    own_s.start()

    for half in range(2):
        for slab in range(NY):
            index = 2 * slab + half
            block = sf[:, index * SLAB:(index + 1) * SLAB].astype(F32)
            sfT[half, slab * SLAB:(slab + 1) * SLAB, :] = jnp.transpose(block).astype(BF16)

    def t_wait(q, kind, index, half=None):
        if half is None:
            region = TW.at[rows_of(index), cols_of(q)]
        else:
            start = pl.multiple_of(q * CHUNK + half * (CHUNK // 2), CHUNK // 2)
            region = TW.at[rows_of(index), pl.ds(start, CHUNK // 2)]
        remote(region, region, t_send, t_recv.at[q, kind], dp=sib).wait_recv()
        return region

    left, right, far = ypeer(3), ypeer(1), ypeer(2)

    @pl.loop(0, NCHUNK)
    def _(q):
        region = t_wait(q, 0, left)
        a = TW.at[rows_of(left), pl.ds(pl.multiple_of(q * CHUNK, CHUNK), CHUNK // 2)]
        remote(a, a, t_send, t_recv.at[q, 2], dp=right).start()
        remote(region, region, t_send, t_recv.at[q, 5], dp=sib).start()
        region = t_wait(q, 1, right)
        b = TW.at[rows_of(right), pl.ds(pl.multiple_of(q * CHUNK + CHUNK // 2, CHUNK // 2), CHUNK // 2)]
        remote(b, b, t_send, t_recv.at[q, 3], dp=left).start()
        remote(region, region, t_send, t_recv.at[q, 6], dp=sib).start()

    mine = SW.at[rows_of(j)]
    for o in (1, 3, 2):
        remote(sw, mine, s_send, s_recv.at[o - 1], dp=ypeer(o)).start()
    remote(sw, mine, s_send, s_recv.at[3], dp=sib).start()
    own_t.wait()
    own_s.wait()

    def logits_chunk(q, feat, W, OUT, top, constant, keep):
        cols = cols_of(q)

        def square(r, acc):
            w = W[pl.ds(pl.multiple_of(r * 16, 16), 16), cols].astype(F32)
            w = w * w
            return acc + (w[:8] + w[8:])

        acc = lax.fori_loop(0, BOTTLE // 16, square, jnp.zeros((8, CHUNK), F32), unroll=4)
        inverse = 1.0 / jnp.sqrt(jnp.sum(acc, axis=0, keepdims=True) + norm_eps)
        if keep is not None:
            keep[:, cols] = jnp.broadcast_to(inverse, (8, CHUNK))
        crow[...] = jnp.broadcast_to(inverse * constant, (8, CHUNK))

        @pl.loop(0, CHUNK // 256)
        def _(b):
            inner = pl.ds(pl.multiple_of(q * CHUNK + b * 256, 256), 256)
            value = jnp.dot(feat[...], W[:, inner], preferred_element_type=F32)
            value = value * crow[0:1, pl.ds(pl.multiple_of(b * 256, 256), 256)]
            OUT[:, inner] = value
            top[...] = jnp.maximum(top[...], jnp.maximum(value[:, :128], value[:, 128:]))

    part[...] = jnp.full((CROPS, LANES), -jnp.inf, F32)
    spart[...] = jnp.full((CROPS, LANES), -jnp.inf, F32)

    def t_far(q):
        t_wait(q, 2, far, 0)
        t_wait(q, 3, far, 1)
        region = TW.at[rows_of(far), cols_of(q)]
        remote(region, region, t_send, t_recv.at[q, 7], dp=sib).start()

    def t_logits(q):
        t_wait(q, 4, sib)
        for kind, o in ((5, 3), (6, 1), (7, 2)):
            t_wait(q, kind, 2 * lax.rem(y + o, NY) + (1 - core))
        logits_chunk(q, tf, TW, Z, part, LOG2E / teacher_temp, None)

    t_far(0)

    @pl.loop(1, NCHUNK)
    def _(q):
        t_far(q)
        t_logits(q - 1)

    t_logits(NCHUNK - 1)

    sent = []

    def exchange(axis, buf, me, n, peer, send, recv):
        slot = buf.at[me]

        @pl.loop(0, n - 1)
        def _(i):
            remote(slot, slot, send, recv, **{axis: peer(i)}).start()

        region = buf.at[pl.ds(0, n - 1)]
        whole = remote(region, region, send, recv, **{axis: peer(0)})
        sent.append(whole)
        return whole.wait_recv

    def over_dp(i, buf):
        return exchange("dp", buf, j, NDP, dpeer, d_send.at[i], d_recv.at[i])

    def over_proto(i, buf):
        return exchange("proto", buf, p, NPR, ppeer, p_send.at[i], p_recv.at[i])

    def combine(buf, n, op):
        total = buf[0]
        for k in range(1, n):
            total = op(total, buf[k])
        return total

    def lane_reduce(part, reduce):
        rows = []
        for i in range(CBLK):
            rows.append(reduce(jnp.transpose(part[i * LANES:(i + 1) * LANES, :]), axis=0, keepdims=True))
        rows.append(jnp.zeros((8 - CBLK, LANES), F32))
        return jnp.concatenate(rows, axis=0)

    def to_columns(value, out):
        for i in range(CBLK):
            out[i * LANES:(i + 1) * LANES, :] = jnp.transpose(jnp.broadcast_to(value[i:i + 1, :], (LANES, LANES)))

    def exp_rows(first, last):
        @pl.loop(first // 8, last // 8)
        def _(r):
            rows = pl.ds(pl.multiple_of(r * 8, 8), 8)
            peak = zcol[rows, :]
            for g in range(GROUPS):
                lanes = pl.ds(g * LANES, LANES)
                Z[rows, lanes] = jnp.exp2(Z[rows, lanes] - peak)

    def proto_pass(out):
        for seg in range(NCHUNK):
            n = CHUNK // LANES

            def step(r, acc):
                rows = pl.ds(pl.multiple_of(r * 8, 8), 8)
                c = ccol[rows, :]
                return tuple(
                    acc[g] + Z[rows, pl.ds(seg * CHUNK + g * LANES, LANES)] * c for g in range(n)
                )

            acc = lax.fori_loop(0, CROPS // 8, step, tuple(jnp.zeros((8, LANES), F32) for _ in range(n)), unroll=8)
            for g in range(n):
                out[pl.ds(seg * n + g, 1), :] = jnp.sum(acc[g], axis=0, keepdims=True)

    def crop_pass():
        @pl.loop(0, CROPS // 32)
        def _(r):
            acc = [jnp.zeros((8, LANES), F32) for _ in range(4)]
            for g in range(GROUPS):
                scale = prow[:, g * LANES:(g + 1) * LANES]
                for k in range(4):
                    rows = pl.ds(pl.multiple_of(r * 32 + k * 8, 8), 8)
                    acc[k] = acc[k] + Z[rows, pl.ds(g * LANES, LANES)] * scale
            for k in range(4):
                part[pl.ds(pl.multiple_of(r * 32 + k * 8, 8), 8), :] = acc[k]

    def crop_loss_pass():
        @pl.loop(0, CROPS // 16)
        def _(r):
            acc = [jnp.zeros((8, LANES), F32) for _ in range(2)]
            acc2 = [jnp.zeros((8, LANES), F32) for _ in range(2)]
            rows = [pl.ds(pl.multiple_of(r * 16 + k * 8, 8), 8) for k in range(2)]
            lse = [lcol[rows[k], :] for k in range(2)]
            for g in range(GROUPS):
                scale = prow[:, g * LANES:(g + 1) * LANES]
                for k in range(2):
                    value = Z[rows[k], pl.ds(g * LANES, LANES)] * scale
                    acc[k] = acc[k] + value
                    acc2[k] = acc2[k] + value * (S[rows[k], pl.ds(g * LANES, LANES)] - lse[k])
            for k in range(2):
                part[rows[k], :] = acc[k]
                spart[rows[k], :] = acc2[k]

    def student_relay():
        for k, o in ((0, 3), (2, 1), (1, 2)):
            region = SW.at[rows_of(ypeer(o))]
            remote(region, region, s_send, s_recv.at[k], dp=sib).wait_recv()
            remote(region, region, s_send, s_recv.at[4 + k], dp=sib).start()

    def student_arrived():
        region = SW.at[rows_of(sib)]
        remote(region, region, s_send, s_recv.at[3], dp=sib).wait_recv()
        for k, o in ((0, 3), (2, 1), (1, 2)):
            region = SW.at[rows_of(2 * lax.rem(y + o, NY) + (1 - core))]
            remote(region, region, s_send, s_recv.at[4 + k], dp=sib).wait_recv()

    def student_chunk(q):
        logits_chunk(q, sf, SW, S, spart, LOG2E / student_temp, isn)

    def student_sums():
        peak = lane_reduce(spart, jnp.max)
        to_columns(peak, lcol)

        @pl.loop(0, CROPS // 8)
        def _(r):
            rows = pl.ds(pl.multiple_of(r * 8, 8), 8)
            top = lcol[rows, :]
            acc = [jnp.zeros((8, LANES), F32) for _ in range(4)]
            for g in range(GROUPS):
                acc[g % 4] = acc[g % 4] + jnp.exp2(S[rows, pl.ds(g * LANES, LANES)] - top)
            spart[rows, :] = (acc[0] + acc[1]) + (acc[2] + acc[3])
        return peak, lane_reduce(spart, jnp.sum)

    own_peak = lane_reduce(part, jnp.max)
    pbuf0[p] = own_peak
    wait = over_proto(0, pbuf0)
    to_columns(own_peak, zcol)
    exp_rows(0, CROPS)
    wait()
    peak = combine(pbuf0, NPR, jnp.maximum)
    adjust = jnp.exp2(own_peak - peak)
    to_columns(adjust, ccol)

    for it in range(ITERS):
        proto_pass(dbuf.at[it, j])
        wait = over_dp(it, dbuf.at[it])
        if it == 0:
            student_relay()
        if it == 1:
            student_chunk(NCHUNK - 1)
            s_peak, s_sum = student_sums()
            pbuf2[p, 8:16] = s_peak
            pbuf2[p, 16:24] = s_sum
        wait()
        pstmp[...] = 1.0 / (TOTAL_PROTOS * combine(dbuf.at[it], NDP, jnp.add))
        for g in range(GROUPS):
            prow[:, g * LANES:(g + 1) * LANES] = jnp.broadcast_to(pstmp[g:g + 1, :], (8, LANES))
        if it < 2:
            crop_pass()
        else:
            crop_loss_pass()
        crop_local = lane_reduce(part, jnp.sum) * adjust
        if it == 0:
            pbuf1[p] = crop_local
            wait = over_proto(1, pbuf1)
            student_arrived()
            for q in range(NCHUNK - 1):
                student_chunk(q)
            wait()
            crop_mass = combine(pbuf1, NPR, jnp.add)
        elif it == 1:
            pbuf2[p, 0:8] = crop_local
            over_proto(2, pbuf2)()
            crop_mass, top = pbuf2[0, 0:8], pbuf2[0, 8:16]
            for k in range(1, NPR):
                crop_mass = crop_mass + pbuf2[k, 0:8]
                top = jnp.maximum(top, pbuf2[k, 8:16])
            total = jnp.zeros((8, LANES), F32)
            for k in range(NPR):
                total = total + pbuf2[k, 16:24] * jnp.exp2(pbuf2[k, 8:16] - top)
            to_columns(top + jnp.log2(total), lcol)
        else:
            pbuf3[p, 0:8] = crop_local
            pbuf3[p, 8:16] = lane_reduce(spart, jnp.sum) * adjust
            over_proto(3, pbuf3)()
            both = combine(pbuf3, NPR, jnp.add)
            crop_mass = both[0:8]
        crop_scale = 1.0 / (TOTAL_CROPS * crop_mass)
        if it < 2:
            to_columns(crop_scale * adjust, ccol)
        else:
            to_columns(crop_scale * adjust * TOTAL_CROPS, ccol)
            crop_loss = (crop_scale * both[8:16])[0:CBLK]
            dbuf4[j, GROUPS:GROUPS + 8] = jnp.concatenate([crop_loss, jnp.zeros((8 - CBLK, LANES), F32)], axis=0)

    def fcols(f):
        return pl.ds(pl.multiple_of(f * FCHUNK, FCHUNK), FCHUNK)

    def sib_copy(f):
        return remote(sendsib.at[:, :, fcols(f)], recvsib.at[:, :, fcols(f)], sib_send, sib_recv.at[f], dp=sib)

    def forward(f):
        sib_copy(f).wait_recv()
        for o in range(1, NY):
            to = lax.rem(y + o, NY)
            total = ownf[to, :, fcols(f)] + recvsib[to, :, fcols(f)].astype(F32)
            sendy[o - 1, :, fcols(f)] = total.astype(BF16)
            remote(
                sendy.at[o - 1, :, fcols(f)], recvy.at[o - 1, :, fcols(f)],
                y_send, y_recv.at[o - 1], dp=ypeer(o),
            ).start()

    @pl.loop(0, NF)
    def _(f):
        scale = jnp.broadcast_to(prow[0:1, fcols(f)], (16, FCHUNK))
        n = FCHUNK // LANES

        def step(r, pressure):
            rows = pl.ds(pl.multiple_of(r * 16, 16), 16)
            c = jnp.concatenate([ccol[rows, :]] * n, axis=1)
            l = jnp.concatenate([lcol[rows, :]] * n, axis=1)
            assign = Z[rows, fcols(f)] * scale * c
            codes[rows, fcols(f)] = assign.astype(BF16)
            s = S[rows, fcols(f)]
            logp = s - l
            signal = ((jnp.exp2(logp) - assign) * (1.0 / student_temp)).astype(BF16)
            sig[rows, :] = signal
            return pressure + signal.astype(F32) * s

        pressure = lax.fori_loop(0, CROPS // 16, step, jnp.zeros((16, FCHUNK), F32), unroll=2)
        pressure = jnp.sum(pressure, axis=0, keepdims=True) * (LN2 * student_temp)
        for g in range(n):
            dbuf4[j, pl.ds(f * n + g, 1), :] = pressure[:, g * LANES:(g + 1) * LANES]
        other = jnp.dot(sfT[1 - core], sig[...], preferred_element_type=F32)
        sendsib[:, :, fcols(f)] = other.astype(BF16).reshape(NY, SLAB, FCHUNK)
        sib_copy(f).start()
        own = jnp.dot(sfT[core], sig[...], preferred_element_type=F32)
        ownf[:, :, fcols(f)] = own.reshape(NY, SLAB, FCHUNK)

        @pl.when(f >= 1)
        def _():
            forward(f - 1)

    wait = over_dp(3, dbuf4)
    forward(NF - 1)
    wait()
    total = combine(dbuf4, NDP, jnp.add)
    pstmp[...] = total[:GROUPS]
    loss_out[0, 0] = jnp.sum(total[GROUPS:]) * (-LN2)

    for o in range(1, NY):
        remote(sendy.at[o - 1], recvy.at[o - 1], y_send, y_recv.at[o - 1], dp=ypeer(o)).wait_recv()

    for f in range(NF):
        cols = slice(f * FCHUNK, (f + 1) * FCHUNK)
        pressure = jnp.concatenate(
            [pstmp[f * 4 + g:f * 4 + g + 1, :] for g in range(FCHUNK // LANES)], axis=1
        )
        inverse = isn[0:1, cols]
        direct = ownf[y, :, cols] + recvsib[y, :, cols].astype(F32)
        for o in range(NY - 1):
            direct = direct + recvy[o, :, cols].astype(F32)
        weight = sw_rows(SW, j, cols).astype(F32)
        grad[:, cols] = (direct - weight * (inverse * pressure)) * inverse

    for whole in sent:
        whole.wait_send()
    region = TW.at[pl.ds(0, 7 * SLAB)]
    remote(region, region, t_send, t_recv.at[0, 0], dp=sib).wait_send()
    region = SW.at[pl.ds(0, 7 * SLAB)]
    remote(region, region, s_send, s_recv.at[0], dp=sib).wait_send()
    remote(sendsib, recvsib, sib_send, sib_recv.at[0], dp=sib).wait_send()
    remote(sendy, recvy, y_send, y_recv.at[0], dp=ypeer(1)).wait_send()


def write_kernel(codes, grad, codes_out, grad_out, code_sem, grad_sem):
    rows = CROPS // NWRITE
    copies = [pltpu.make_async_copy(grad, grad_out, grad_sem)]
    for i in range(NWRITE):
        part = pl.ds(i * rows, rows)
        copies.append(pltpu.make_async_copy(codes.at[part], codes_out.at[part], code_sem.at[i]))
    for copy in copies:
        copy.start()
    for copy in copies:
        copy.wait()


def sw_rows(SW, j, cols):
    return SW[pl.ds(pl.multiple_of(j * SLAB, 16), SLAB), cols]


def body(teacher_features, student_features, teacher_weight, student_weight):
    vmem = pl.BlockSpec(memory_space=pltpu.VMEM)
    hbm = pl.BlockSpec(memory_space=pl.ANY)
    dma = pltpu.SemaphoreType.DMA
    codes, loss, grad = pl.pallas_call(
        head_kernel,
        out_shape=(
            pltpu.VMEM((CROPS, PROTOS), BF16),
            jax.ShapeDtypeStruct((1, 1), F32),
            pltpu.VMEM((SLAB, PROTOS), F32),
        ),
        in_specs=[vmem, vmem, hbm, hbm],
        out_specs=(vmem, pl.BlockSpec(memory_space=pltpu.SMEM), vmem),
        scratch_shapes=[
            pltpu.VMEM((BOTTLE, PROTOS), BF16),
            pltpu.VMEM((BOTTLE, PROTOS), BF16),
            pltpu.VMEM((CROPS, PROTOS), F32),
            pltpu.VMEM((CROPS, PROTOS), F32),
            pltpu.VMEM((2, BOTTLE // 2, CROPS), BF16),
            pltpu.VMEM((CROPS, LANES), F32),
            pltpu.VMEM((CROPS, LANES), F32),
            pltpu.VMEM((CROPS, LANES), F32),
            pltpu.VMEM((CROPS, LANES), F32),
            pltpu.VMEM((CROPS, LANES), F32),
            pltpu.VMEM((8, CHUNK), F32),
            pltpu.VMEM((8, PROTOS), F32),
            pltpu.VMEM((GROUPS, LANES), F32),
            pltpu.VMEM((8, PROTOS), F32),
            pltpu.VMEM((CROPS, FCHUNK), BF16),
            pltpu.VMEM((NY, SLAB, PROTOS), F32),
            pltpu.VMEM((NY, SLAB, PROTOS), BF16),
            pltpu.VMEM((NY, SLAB, PROTOS), BF16),
            pltpu.VMEM((NY - 1, SLAB, PROTOS), BF16),
            pltpu.VMEM((NY - 1, SLAB, PROTOS), BF16),
            pltpu.VMEM((ITERS, NDP, GROUPS, LANES), F32),
            pltpu.VMEM((NDP, GROUPS + 8, LANES), F32),
            pltpu.VMEM((NPR, 8, LANES), F32),
            pltpu.VMEM((NPR, 8, LANES), F32),
            pltpu.VMEM((NPR, 24, LANES), F32),
            pltpu.VMEM((NPR, 16, LANES), F32),
            dma((2,)), dma, dma((NCHUNK, 8)), dma, dma((7,)),
            dma((4,)), dma((4,)), dma((4,)), dma((4,)),
            dma, dma((NF,)), dma, dma((NY - 1,)),
        ],
        compiler_params=pltpu.CompilerParams(
            collective_id=0, has_side_effects=True, vmem_limit_bytes=52 * 1024 * 1024
        ),
    )(teacher_features, student_features, teacher_weight, student_weight)
    codes, grad = pl.pallas_call(
        write_kernel,
        out_shape=(
            jax.ShapeDtypeStruct((CROPS, PROTOS), BF16),
            jax.ShapeDtypeStruct((SLAB, PROTOS), F32),
        ),
        in_specs=[vmem, vmem],
        out_specs=(hbm, hbm),
        scratch_shapes=[dma((NWRITE,)), dma],
        compiler_params=pltpu.CompilerParams(vmem_limit_bytes=1024 * 1024),
    )(codes, grad)
    return codes, loss[0, 0], grad


def solution(mesh):
    return jax.shard_map(
        body,
        mesh=mesh,
        in_specs=(P("dp", None), P("dp", None), P("dp", "proto"), P("dp", "proto")),
        out_specs=(P("dp", "proto"), P(), P("dp", "proto")),
        check_vma=False,
    )
```

```python
import math

import jax
import jax.numpy as jnp
from jax import lax
from jax.experimental import pallas as pl
from jax.experimental.pallas import tpu as pltpu
from jax.sharding import PartitionSpec as P

ITERS = 3
teacher_temp = 0.07
student_temp = 0.1
norm_eps = 1e-06
MESH = pl.DeviceIdType.MESH
LOG2E = math.log2(math.e)
LN2 = math.log(2.0)
F32 = jnp.float32
BF16 = jnp.bfloat16

NY, NX, NZ = 4, 4, 8
NDP = 2 * NY
NPR = NX * NZ
CROPS = 768
PROTOS = 4096
BOTTLE = 384
SLAB = BOTTLE // NDP
LANES = 128
GROUPS = PROTOS // LANES
CBLK = CROPS // LANES
NCHUNK = 4
CHUNK = PROTOS // NCHUNK
FCHUNK = 512
NF = PROTOS // FCHUNK
NWRITE = 4
TOTAL_CROPS = CROPS * NDP
TOTAL_PROTOS = PROTOS * NPR


def remote(src, dst, send, recv, **device):
    return pltpu.make_async_remote_copy(
        src_ref=src, dst_ref=dst, send_sem=send, recv_sem=recv, device_id=device, device_id_type=MESH
    )


def head_kernel(
    tf, sf, tw, sw,
    codes, loss_out, grad,
    TW, SW, Z, S, sfT, part, spart, zcol, ccol, lcol, crow, prow, pstmp, isn,
    sig, ownf, sendsib, recvsib, sendy, recvy,
    dbuf, dbuf4, pbuf0, pbuf1, pbuf2, pbuf3,
    local_sem, t_send, t_recv, s_send, s_recv,
    d_send, d_recv, p_send, p_recv, sib_send, sib_recv, y_send, y_recv,
):
    j = lax.axis_index("dp")
    p = lax.axis_index("proto")
    y, core = lax.div(j, 2), lax.rem(j, 2)
    z, x = lax.div(p, NX), lax.rem(p, NX)
    sib = 2 * y + (1 - core)

    def ypeer(o):
        return 2 * lax.rem(y + o, NY) + core

    def swing(i, n):
        return n // 2 + lax.div(i + 1, 2) * (1 - 2 * lax.rem(i, 2))

    def dpeer(i):
        return 2 * lax.rem(y + swing(lax.div(i, 2), NY), NY) + lax.rem(core + 1 + i, 2)

    def ppeer(i):
        return lax.rem(z + swing(lax.div(i, NX), NZ), NZ) * NX + lax.rem(x + 1 + i, NX)

    barrier = pltpu.get_barrier_semaphore()

    @pl.loop(0, NPR - 1)
    def _(i):
        pl.semaphore_signal(barrier, inc=1, device_id={"proto": ppeer(i)}, device_id_type=MESH)

    @pl.loop(0, NDP - 1)
    def _(i):
        pl.semaphore_signal(barrier, inc=1, device_id={"dp": dpeer(i)}, device_id_type=MESH)

    pl.semaphore_wait(barrier, (NDP - 1) + (NPR - 1))

    def rows_of(index):
        return pl.ds(pl.multiple_of(index * SLAB, 16), SLAB)

    def cols_of(q):
        return pl.ds(pl.multiple_of(q * CHUNK, CHUNK), CHUNK)

    @pl.loop(0, NCHUNK)
    def _(q):
        src = tw.at[:, cols_of(q)]
        dst = TW.at[rows_of(j), cols_of(q)]
        remote(src, dst, t_send, t_recv.at[q, 0], dp=ypeer(1)).start()
        remote(src, dst, t_send, t_recv.at[q, 1], dp=ypeer(3)).start()
        remote(src, dst, t_send, t_recv.at[q, 4], dp=sib).start()

    own_t = pltpu.make_async_copy(tw, TW.at[rows_of(j)], local_sem.at[0])
    own_s = pltpu.make_async_copy(sw, SW.at[rows_of(j)], local_sem.at[1])
    own_t.start()
    own_s.start()

    for half in range(2):
        for slab in range(NY):
            index = 2 * slab + half
            block = sf[:, index * SLAB:(index + 1) * SLAB].astype(F32)
            sfT[half, slab * SLAB:(slab + 1) * SLAB, :] = jnp.transpose(block).astype(BF16)

    def t_wait(q, kind, index, half=None):
        if half is None:
            region = TW.at[rows_of(index), cols_of(q)]
        else:
            start = pl.multiple_of(q * CHUNK + half * (CHUNK // 2), CHUNK // 2)
            region = TW.at[rows_of(index), pl.ds(start, CHUNK // 2)]
        remote(region, region, t_send, t_recv.at[q, kind], dp=sib).wait_recv()
        return region

    left, right, far = ypeer(3), ypeer(1), ypeer(2)

    @pl.loop(0, NCHUNK)
    def _(q):
        region = t_wait(q, 0, left)
        a = TW.at[rows_of(left), pl.ds(pl.multiple_of(q * CHUNK, CHUNK), CHUNK // 2)]
        remote(a, a, t_send, t_recv.at[q, 2], dp=right).start()
        remote(region, region, t_send, t_recv.at[q, 5], dp=sib).start()
        region = t_wait(q, 1, right)
        b = TW.at[rows_of(right), pl.ds(pl.multiple_of(q * CHUNK + CHUNK // 2, CHUNK // 2), CHUNK // 2)]
        remote(b, b, t_send, t_recv.at[q, 3], dp=left).start()
        remote(region, region, t_send, t_recv.at[q, 6], dp=sib).start()

    mine = SW.at[rows_of(j)]
    for o in (1, 3, 2):
        remote(sw, mine, s_send, s_recv.at[o - 1], dp=ypeer(o)).start()
    remote(sw, mine, s_send, s_recv.at[3], dp=sib).start()
    own_t.wait()
    own_s.wait()

    def logits_chunk(q, feat, W, OUT, top, constant, keep):
        cols = cols_of(q)

        def square(r, acc):
            w = W[pl.ds(pl.multiple_of(r * 16, 16), 16), cols].astype(F32)
            w = w * w
            return acc + (w[:8] + w[8:])

        acc = lax.fori_loop(0, BOTTLE // 16, square, jnp.zeros((8, CHUNK), F32), unroll=4)
        inverse = 1.0 / jnp.sqrt(jnp.sum(acc, axis=0, keepdims=True) + norm_eps)
        if keep is not None:
            keep[:, cols] = jnp.broadcast_to(inverse, (8, CHUNK))
        crow[...] = jnp.broadcast_to(inverse * constant, (8, CHUNK))

        @pl.loop(0, CHUNK // 256)
        def _(b):
            inner = pl.ds(pl.multiple_of(q * CHUNK + b * 256, 256), 256)
            value = jnp.dot(feat[...], W[:, inner], preferred_element_type=F32)
            value = value * crow[0:1, pl.ds(pl.multiple_of(b * 256, 256), 256)]
            OUT[:, inner] = value
            top[...] = jnp.maximum(top[...], jnp.maximum(value[:, :128], value[:, 128:]))

    part[...] = jnp.full((CROPS, LANES), -jnp.inf, F32)
    spart[...] = jnp.full((CROPS, LANES), -jnp.inf, F32)

    def t_far(q):
        t_wait(q, 2, far, 0)
        t_wait(q, 3, far, 1)
        region = TW.at[rows_of(far), cols_of(q)]
        remote(region, region, t_send, t_recv.at[q, 7], dp=sib).start()

    def t_logits(q):
        t_wait(q, 4, sib)
        for kind, o in ((5, 3), (6, 1), (7, 2)):
            t_wait(q, kind, 2 * lax.rem(y + o, NY) + (1 - core))
        logits_chunk(q, tf, TW, Z, part, LOG2E / teacher_temp, None)

    t_far(0)

    @pl.loop(1, NCHUNK)
    def _(q):
        t_far(q)
        t_logits(q - 1)

    t_logits(NCHUNK - 1)

    sent = []

    def exchange(axis, buf, me, n, peer, send, recv):
        slot = buf.at[me]

        @pl.loop(0, n - 1)
        def _(i):
            remote(slot, slot, send, recv, **{axis: peer(i)}).start()

        region = buf.at[pl.ds(0, n - 1)]
        whole = remote(region, region, send, recv, **{axis: peer(0)})
        sent.append(whole)
        return whole.wait_recv

    def over_dp(i, buf):
        return exchange("dp", buf, j, NDP, dpeer, d_send.at[i], d_recv.at[i])

    def over_proto(i, buf):
        return exchange("proto", buf, p, NPR, ppeer, p_send.at[i], p_recv.at[i])

    def combine(buf, n, op):
        total = buf[0]
        for k in range(1, n):
            total = op(total, buf[k])
        return total

    def lane_reduce(part, reduce):
        rows = []
        for i in range(CBLK):
            rows.append(reduce(jnp.transpose(part[i * LANES:(i + 1) * LANES, :]), axis=0, keepdims=True))
        rows.append(jnp.zeros((8 - CBLK, LANES), F32))
        return jnp.concatenate(rows, axis=0)

    def to_columns(value, out):
        for i in range(CBLK):
            out[i * LANES:(i + 1) * LANES, :] = jnp.transpose(jnp.broadcast_to(value[i:i + 1, :], (LANES, LANES)))

    def exp_rows(first, last):
        @pl.loop(first // 8, last // 8)
        def _(r):
            rows = pl.ds(pl.multiple_of(r * 8, 8), 8)
            peak = zcol[rows, :]
            for g in range(GROUPS):
                lanes = pl.ds(g * LANES, LANES)
                Z[rows, lanes] = jnp.exp2(Z[rows, lanes] - peak)

    def proto_pass(out):
        for seg in range(NCHUNK):
            n = CHUNK // LANES

            def step(r, acc):
                rows = pl.ds(pl.multiple_of(r * 8, 8), 8)
                c = ccol[rows, :]
                return tuple(
                    acc[g] + Z[rows, pl.ds(seg * CHUNK + g * LANES, LANES)] * c for g in range(n)
                )

            acc = lax.fori_loop(0, CROPS // 8, step, tuple(jnp.zeros((8, LANES), F32) for _ in range(n)), unroll=8)
            for g in range(n):
                out[pl.ds(seg * n + g, 1), :] = jnp.sum(acc[g], axis=0, keepdims=True)

    def crop_pass():
        @pl.loop(0, CROPS // 32)
        def _(r):
            acc = [jnp.zeros((8, LANES), F32) for _ in range(4)]
            for g in range(GROUPS):
                scale = prow[:, g * LANES:(g + 1) * LANES]
                for k in range(4):
                    rows = pl.ds(pl.multiple_of(r * 32 + k * 8, 8), 8)
                    acc[k] = acc[k] + Z[rows, pl.ds(g * LANES, LANES)] * scale
            for k in range(4):
                part[pl.ds(pl.multiple_of(r * 32 + k * 8, 8), 8), :] = acc[k]

    def crop_loss_pass():
        @pl.loop(0, CROPS // 16)
        def _(r):
            acc = [jnp.zeros((8, LANES), F32) for _ in range(2)]
            acc2 = [jnp.zeros((8, LANES), F32) for _ in range(2)]
            rows = [pl.ds(pl.multiple_of(r * 16 + k * 8, 8), 8) for k in range(2)]
            lse = [lcol[rows[k], :] for k in range(2)]
            for g in range(GROUPS):
                scale = prow[:, g * LANES:(g + 1) * LANES]
                for k in range(2):
                    value = Z[rows[k], pl.ds(g * LANES, LANES)] * scale
                    acc[k] = acc[k] + value
                    acc2[k] = acc2[k] + value * (S[rows[k], pl.ds(g * LANES, LANES)] - lse[k])
            for k in range(2):
                part[rows[k], :] = acc[k]
                spart[rows[k], :] = acc2[k]

    def student_relay():
        for k, o in ((0, 3), (2, 1), (1, 2)):
            region = SW.at[rows_of(ypeer(o))]
            remote(region, region, s_send, s_recv.at[k], dp=sib).wait_recv()
            remote(region, region, s_send, s_recv.at[4 + k], dp=sib).start()

    def student_arrived():
        region = SW.at[rows_of(sib)]
        remote(region, region, s_send, s_recv.at[3], dp=sib).wait_recv()
        for k, o in ((0, 3), (2, 1), (1, 2)):
            region = SW.at[rows_of(2 * lax.rem(y + o, NY) + (1 - core))]
            remote(region, region, s_send, s_recv.at[4 + k], dp=sib).wait_recv()

    def student_chunk(q):
        logits_chunk(q, sf, SW, S, spart, LOG2E / student_temp, isn)

    def student_sums():
        peak = lane_reduce(spart, jnp.max)
        to_columns(peak, lcol)

        @pl.loop(0, CROPS // 8)
        def _(r):
            rows = pl.ds(pl.multiple_of(r * 8, 8), 8)
            top = lcol[rows, :]
            acc = [jnp.zeros((8, LANES), F32) for _ in range(4)]
            for g in range(GROUPS):
                acc[g % 4] = acc[g % 4] + jnp.exp2(S[rows, pl.ds(g * LANES, LANES)] - top)
            spart[rows, :] = (acc[0] + acc[1]) + (acc[2] + acc[3])
        return peak, lane_reduce(spart, jnp.sum)

    own_peak = lane_reduce(part, jnp.max)
    pbuf0[p] = own_peak
    wait = over_proto(0, pbuf0)
    to_columns(own_peak, zcol)
    exp_rows(0, CROPS)
    wait()
    peak = combine(pbuf0, NPR, jnp.maximum)
    adjust = jnp.exp2(own_peak - peak)
    to_columns(adjust, ccol)

    for it in range(ITERS):
        proto_pass(dbuf.at[it, j])
        wait = over_dp(it, dbuf.at[it])
        if it == 0:
            student_relay()
        if it == 1:
            student_chunk(NCHUNK - 1)
            s_peak, s_sum = student_sums()
            pbuf2[p, 8:16] = s_peak
            pbuf2[p, 16:24] = s_sum
        wait()
        pstmp[...] = 1.0 / (TOTAL_PROTOS * combine(dbuf.at[it], NDP, jnp.add))
        for g in range(GROUPS):
            prow[:, g * LANES:(g + 1) * LANES] = jnp.broadcast_to(pstmp[g:g + 1, :], (8, LANES))
        if it < 2:
            crop_pass()
        else:
            crop_loss_pass()
        crop_local = lane_reduce(part, jnp.sum) * adjust
        if it == 0:
            pbuf1[p] = crop_local
            wait = over_proto(1, pbuf1)
            student_arrived()
            for q in range(NCHUNK - 1):
                student_chunk(q)
            wait()
            crop_mass = combine(pbuf1, NPR, jnp.add)
        elif it == 1:
            pbuf2[p, 0:8] = crop_local
            over_proto(2, pbuf2)()
            crop_mass, top = pbuf2[0, 0:8], pbuf2[0, 8:16]
            for k in range(1, NPR):
                crop_mass = crop_mass + pbuf2[k, 0:8]
                top = jnp.maximum(top, pbuf2[k, 8:16])
            total = jnp.zeros((8, LANES), F32)
            for k in range(NPR):
                total = total + pbuf2[k, 16:24] * jnp.exp2(pbuf2[k, 8:16] - top)
            to_columns(top + jnp.log2(total), lcol)
        else:
            pbuf3[p, 0:8] = crop_local
            pbuf3[p, 8:16] = lane_reduce(spart, jnp.sum) * adjust
            over_proto(3, pbuf3)()
            both = combine(pbuf3, NPR, jnp.add)
            crop_mass = both[0:8]
        crop_scale = 1.0 / (TOTAL_CROPS * crop_mass)
        if it < 2:
            to_columns(crop_scale * adjust, ccol)
        else:
            to_columns(crop_scale * adjust * TOTAL_CROPS, ccol)
            crop_loss = (crop_scale * both[8:16])[0:CBLK]
            dbuf4[j, GROUPS:GROUPS + 8] = jnp.concatenate([crop_loss, jnp.zeros((8 - CBLK, LANES), F32)], axis=0)

    def fcols(f):
        return pl.ds(pl.multiple_of(f * FCHUNK, FCHUNK), FCHUNK)

    def sib_copy(f):
        return remote(sendsib.at[:, :, fcols(f)], recvsib.at[:, :, fcols(f)], sib_send, sib_recv.at[f], dp=sib)

    def via(f):
        return jnp.where(lax.rem(f, 2) == 0, right, left), jnp.where(lax.rem(f, 2) == 0, left, right)

    def y_copy(f, kind, to):
        return remote(
            sendy.at[kind, :, fcols(f)], recvy.at[kind, :, fcols(f)], y_send, y_recv.at[kind, f], dp=to
        )

    def chip_sum(index, f):
        slab = lax.div(index, 2)
        return ownf[slab, :, fcols(f)] + recvsib[slab, :, fcols(f)]

    def forward(f):
        sib_copy(f).wait_recv()
        near, away = via(f)
        sendy[0, :, fcols(f)] = chip_sum(far, f).astype(BF16)
        y_copy(f, 0, near).start()
        sendy[1, :, fcols(f)] = chip_sum(away, f).astype(BF16)
        y_copy(f, 1, away).start()

    def forward_direct(f):
        sib_copy(f).wait_recv()
        near, away = via(f)
        for kind, to in ((0, far), (1, away), (2, near)):
            sendy[kind, :, fcols(f)] = chip_sum(to, f).astype(BF16)
            y_copy(f, kind, to).start()

    def pass_on(f):
        near, away = via(f)
        y_copy(f, 0, near).wait_recv()
        sendy[2, :, fcols(f)] = (chip_sum(near, f) + recvy[0, :, fcols(f)].astype(F32)).astype(BF16)
        y_copy(f, 2, near).start()

    @pl.loop(0, NF)
    def _(f):
        scale = jnp.broadcast_to(prow[0:1, fcols(f)], (16, FCHUNK))
        n = FCHUNK // LANES

        def step(r, pressure):
            rows = pl.ds(pl.multiple_of(r * 16, 16), 16)
            c = jnp.concatenate([ccol[rows, :]] * n, axis=1)
            l = jnp.concatenate([lcol[rows, :]] * n, axis=1)
            assign = Z[rows, fcols(f)] * scale * c
            codes[rows, fcols(f)] = assign.astype(BF16)
            s = S[rows, fcols(f)]
            logp = s - l
            signal = ((jnp.exp2(logp) - assign) * (1.0 / student_temp)).astype(BF16)
            sig[rows, :] = signal
            return pressure + signal.astype(F32) * s

        pressure = lax.fori_loop(0, CROPS // 16, step, jnp.zeros((16, FCHUNK), F32), unroll=2)
        pressure = jnp.sum(pressure, axis=0, keepdims=True) * (LN2 * student_temp)
        for g in range(n):
            dbuf4[j, pl.ds(f * n + g, 1), :] = pressure[:, g * LANES:(g + 1) * LANES]
        other = jnp.dot(sfT[1 - core], sig[...], preferred_element_type=F32)
        sendsib[:, :, fcols(f)] = other.reshape(NY, SLAB, FCHUNK)
        sib_copy(f).start()
        own = jnp.dot(sfT[core], sig[...], preferred_element_type=F32)
        ownf[:, :, fcols(f)] = own.reshape(NY, SLAB, FCHUNK)

        @pl.when(f >= 2)
        def _():
            forward(f - 2)

        @pl.when(f >= 4)
        def _():
            pass_on(f - 4)

    wait = over_dp(3, dbuf4)
    forward_direct(NF - 2)
    pass_on(NF - 4)
    forward_direct(NF - 1)
    pass_on(NF - 3)
    wait()
    total = combine(dbuf4, NDP, jnp.add)
    pstmp[...] = total[:GROUPS]
    loss_out[0, 0] = jnp.sum(total[GROUPS:]) * (-LN2)

    for f in range(NF):
        cols = slice(f * FCHUNK, (f + 1) * FCHUNK)
        y_copy(f, 1, left).wait_recv()
        y_copy(f, 2, left).wait_recv()
        pressure = jnp.concatenate(
            [pstmp[f * 4 + g:f * 4 + g + 1, :] for g in range(FCHUNK // LANES)], axis=1
        )
        inverse = isn[0:1, cols]
        direct = ownf[y, :, cols] + recvsib[y, :, cols]
        direct = direct + (recvy[1, :, cols].astype(F32) + recvy[2, :, cols].astype(F32))
        if f >= NF - 2:
            y_copy(f, 0, left).wait_recv()
            direct = direct + recvy[0, :, cols].astype(F32)
        weight = sw_rows(SW, j, cols).astype(F32)
        grad[:, cols] = (direct - weight * (inverse * pressure)) * inverse

    for whole in sent:
        whole.wait_send()
    region = TW.at[pl.ds(0, 7 * SLAB)]
    remote(region, region, t_send, t_recv.at[0, 0], dp=sib).wait_send()
    region = SW.at[pl.ds(0, 7 * SLAB)]
    remote(region, region, s_send, s_recv.at[0], dp=sib).wait_send()
    remote(sendsib, recvsib, sib_send, sib_recv.at[0], dp=sib).wait_send()
    remote(sendy, recvy, y_send, y_recv.at[0, 0], dp=right).wait_send()


def write_kernel(codes, grad, codes_out, grad_out, code_sem, grad_sem):
    rows = CROPS // NWRITE
    copies = [pltpu.make_async_copy(grad, grad_out, grad_sem)]
    for i in range(NWRITE):
        part = pl.ds(i * rows, rows)
        copies.append(pltpu.make_async_copy(codes.at[part], codes_out.at[part], code_sem.at[i]))
    for copy in copies:
        copy.start()
    for copy in copies:
        copy.wait()


def sw_rows(SW, j, cols):
    return SW[pl.ds(pl.multiple_of(j * SLAB, 16), SLAB), cols]


def body(teacher_features, student_features, teacher_weight, student_weight):
    vmem = pl.BlockSpec(memory_space=pltpu.VMEM)
    hbm = pl.BlockSpec(memory_space=pl.ANY)
    dma = pltpu.SemaphoreType.DMA
    codes, loss, grad = pl.pallas_call(
        head_kernel,
        out_shape=(
            pltpu.VMEM((CROPS, PROTOS), BF16),
            jax.ShapeDtypeStruct((1, 1), F32),
            pltpu.VMEM((SLAB, PROTOS), F32),
        ),
        in_specs=[vmem, vmem, hbm, hbm],
        out_specs=(vmem, pl.BlockSpec(memory_space=pltpu.SMEM), vmem),
        scratch_shapes=[
            pltpu.VMEM((BOTTLE, PROTOS), BF16),
            pltpu.VMEM((BOTTLE, PROTOS), BF16),
            pltpu.VMEM((CROPS, PROTOS), F32),
            pltpu.VMEM((CROPS, PROTOS), F32),
            pltpu.VMEM((2, BOTTLE // 2, CROPS), BF16),
            pltpu.VMEM((CROPS, LANES), F32),
            pltpu.VMEM((CROPS, LANES), F32),
            pltpu.VMEM((CROPS, LANES), F32),
            pltpu.VMEM((CROPS, LANES), F32),
            pltpu.VMEM((CROPS, LANES), F32),
            pltpu.VMEM((8, CHUNK), F32),
            pltpu.VMEM((8, PROTOS), F32),
            pltpu.VMEM((GROUPS, LANES), F32),
            pltpu.VMEM((8, PROTOS), F32),
            pltpu.VMEM((CROPS, FCHUNK), BF16),
            pltpu.VMEM((NY, SLAB, PROTOS), F32),
            pltpu.VMEM((NY, SLAB, PROTOS), F32),
            pltpu.VMEM((NY, SLAB, PROTOS), F32),
            pltpu.VMEM((NY - 1, SLAB, PROTOS), BF16),
            pltpu.VMEM((NY - 1, SLAB, PROTOS), BF16),
            pltpu.VMEM((ITERS, NDP, GROUPS, LANES), F32),
            pltpu.VMEM((NDP, GROUPS + 8, LANES), F32),
            pltpu.VMEM((NPR, 8, LANES), F32),
            pltpu.VMEM((NPR, 8, LANES), F32),
            pltpu.VMEM((NPR, 24, LANES), F32),
            pltpu.VMEM((NPR, 16, LANES), F32),
            dma((2,)), dma, dma((NCHUNK, 8)), dma, dma((7,)),
            dma((4,)), dma((4,)), dma((4,)), dma((4,)),
            dma, dma((NF,)), dma, dma((NY - 1, NF)),
        ],
        compiler_params=pltpu.CompilerParams(
            collective_id=0, has_side_effects=True, vmem_limit_bytes=54 * 1024 * 1024
        ),
    )(teacher_features, student_features, teacher_weight, student_weight)
    codes, grad = pl.pallas_call(
        write_kernel,
        out_shape=(
            jax.ShapeDtypeStruct((CROPS, PROTOS), BF16),
            jax.ShapeDtypeStruct((SLAB, PROTOS), F32),
        ),
        in_specs=[vmem, vmem],
        out_specs=(hbm, hbm),
        scratch_shapes=[dma((NWRITE,)), dma],
        compiler_params=pltpu.CompilerParams(vmem_limit_bytes=1024 * 1024),
    )(codes, grad)
    return codes, loss[0, 0], grad


def solution(mesh):
    return jax.shard_map(
        body,
        mesh=mesh,
        in_specs=(P("dp", None), P("dp", None), P("dp", "proto"), P("dp", "proto")),
        out_specs=(P("dp", "proto"), P(), P("dp", "proto")),
        check_vma=False,
    )
```

```python
import math

import jax
import jax.numpy as jnp
from jax import lax
from jax.experimental import pallas as pl
from jax.experimental.pallas import tpu as pltpu
from jax.sharding import PartitionSpec as P

ITERS = 3
teacher_temp = 0.07
student_temp = 0.1
norm_eps = 1e-06
MESH = pl.DeviceIdType.MESH
LOG2E = math.log2(math.e)
LN2 = math.log(2.0)
F32 = jnp.float32
BF16 = jnp.bfloat16

NY, NX, NZ = 4, 4, 8
NDP = 2 * NY
NPR = NX * NZ
CROPS = 768
PROTOS = 4096
BOTTLE = 384
SLAB = BOTTLE // NDP
LANES = 128
GROUPS = PROTOS // LANES
CBLK = CROPS // LANES
NCHUNK = 4
CHUNK = PROTOS // NCHUNK
FCHUNK = 512
NF = PROTOS // FCHUNK
NWRITE = 4
TOTAL_CROPS = CROPS * NDP
TOTAL_PROTOS = PROTOS * NPR


def remote(src, dst, send, recv, **device):
    return pltpu.make_async_remote_copy(
        src_ref=src, dst_ref=dst, send_sem=send, recv_sem=recv, device_id=device, device_id_type=MESH
    )


def head_kernel(
    tf, sf, tw, sw,
    codes, loss_out, grad,
    TW, SW, Z, S, sfT, part, spart, zcol, ccol, lcol, crow, prow, pstmp, isn,
    sig, ownf, sendsib, recvsib, sendy, recvy,
    dbuf, dbuf4, pbuf0, pbuf1, pbuf2, pbuf3,
    local_sem, t_send, t_recv, s_send, s_recv,
    d_send, d_recv, p_send, p_recv, sib_send, sib_recv, y_send, y_recv,
):
    j = lax.axis_index("dp")
    p = lax.axis_index("proto")
    y, core = lax.div(j, 2), lax.rem(j, 2)
    z, x = lax.div(p, NX), lax.rem(p, NX)
    sib = 2 * y + (1 - core)

    def ypeer(o):
        return 2 * lax.rem(y + o, NY) + core

    def swing(i, n):
        return n // 2 + lax.div(i + 1, 2) * (1 - 2 * lax.rem(i, 2))

    def dpeer(i):
        return 2 * lax.rem(y + swing(lax.div(i, 2), NY), NY) + lax.rem(core + 1 + i, 2)

    def ppeer(i):
        return lax.rem(z + swing(lax.div(i, NX), NZ), NZ) * NX + lax.rem(x + 1 + i, NX)

    barrier = pltpu.get_barrier_semaphore()

    @pl.loop(0, NPR - 1)
    def _(i):
        pl.semaphore_signal(barrier, inc=1, device_id={"proto": ppeer(i)}, device_id_type=MESH)

    @pl.loop(0, NDP - 1)
    def _(i):
        pl.semaphore_signal(barrier, inc=1, device_id={"dp": dpeer(i)}, device_id_type=MESH)

    pl.semaphore_wait(barrier, (NDP - 1) + (NPR - 1))

    def rows_of(index):
        return pl.ds(pl.multiple_of(index * SLAB, 16), SLAB)

    def cols_of(q):
        return pl.ds(pl.multiple_of(q * CHUNK, CHUNK), CHUNK)

    @pl.loop(0, NCHUNK)
    def _(q):
        src = tw.at[:, cols_of(q)]
        dst = TW.at[rows_of(j), cols_of(q)]
        remote(src, dst, t_send, t_recv.at[q, 0], dp=ypeer(1)).start()
        remote(src, dst, t_send, t_recv.at[q, 1], dp=ypeer(3)).start()
        remote(src, dst, t_send, t_recv.at[q, 4], dp=sib).start()

    own_t = pltpu.make_async_copy(tw, TW.at[rows_of(j)], local_sem.at[0])
    own_s = pltpu.make_async_copy(sw, SW.at[rows_of(j)], local_sem.at[1])
    own_t.start()
    own_s.start()

    for half in range(2):
        for slab in range(NY):
            index = 2 * slab + half
            block = sf[:, index * SLAB:(index + 1) * SLAB].astype(F32)
            sfT[half, slab * SLAB:(slab + 1) * SLAB, :] = jnp.transpose(block).astype(BF16)

    def t_wait(q, kind, index, half=None):
        if half is None:
            region = TW.at[rows_of(index), cols_of(q)]
        else:
            start = pl.multiple_of(q * CHUNK + half * (CHUNK // 2), CHUNK // 2)
            region = TW.at[rows_of(index), pl.ds(start, CHUNK // 2)]
        remote(region, region, t_send, t_recv.at[q, kind], dp=sib).wait_recv()
        return region

    left, right, far = ypeer(3), ypeer(1), ypeer(2)

    @pl.loop(0, NCHUNK)
    def _(q):
        region = t_wait(q, 0, left)
        a = TW.at[rows_of(left), pl.ds(pl.multiple_of(q * CHUNK, CHUNK), CHUNK // 2)]
        remote(a, a, t_send, t_recv.at[q, 2], dp=right).start()
        remote(region, region, t_send, t_recv.at[q, 5], dp=sib).start()
        region = t_wait(q, 1, right)
        b = TW.at[rows_of(right), pl.ds(pl.multiple_of(q * CHUNK + CHUNK // 2, CHUNK // 2), CHUNK // 2)]
        remote(b, b, t_send, t_recv.at[q, 3], dp=left).start()
        remote(region, region, t_send, t_recv.at[q, 6], dp=sib).start()

    mine = SW.at[rows_of(j)]
    for o in (1, 3, 2):
        remote(sw, mine, s_send, s_recv.at[o - 1], dp=ypeer(o)).start()
    remote(sw, mine, s_send, s_recv.at[3], dp=sib).start()
    own_t.wait()
    own_s.wait()

    def logits_chunk(q, feat, W, OUT, top, constant, keep):
        cols = cols_of(q)

        def square(r, acc):
            w = W[pl.ds(pl.multiple_of(r * 16, 16), 16), cols].astype(F32)
            w = w * w
            return acc + (w[:8] + w[8:])

        acc = lax.fori_loop(0, BOTTLE // 16, square, jnp.zeros((8, CHUNK), F32), unroll=4)
        inverse = 1.0 / jnp.sqrt(jnp.sum(acc, axis=0, keepdims=True) + norm_eps)
        if keep is not None:
            keep[:, cols] = jnp.broadcast_to(inverse, (8, CHUNK))
        crow[...] = jnp.broadcast_to(inverse * constant, (8, CHUNK))

        @pl.loop(0, CHUNK // 256, unroll=2)
        def _(b):
            inner = pl.ds(pl.multiple_of(q * CHUNK + b * 256, 256), 256)
            value = jnp.dot(feat[...], W[:, inner], preferred_element_type=F32)
            value = value * crow[0:1, pl.ds(pl.multiple_of(b * 256, 256), 256)]
            OUT[:, inner] = value
            top[...] = jnp.maximum(top[...], jnp.maximum(value[:, :128], value[:, 128:]))

    part[...] = jnp.full((CROPS, LANES), -jnp.inf, F32)
    spart[...] = jnp.full((CROPS, LANES), -jnp.inf, F32)

    def t_far(q):
        t_wait(q, 2, far, 0)
        t_wait(q, 3, far, 1)
        region = TW.at[rows_of(far), cols_of(q)]
        remote(region, region, t_send, t_recv.at[q, 7], dp=sib).start()

    def t_logits(q):
        t_wait(q, 4, sib)
        for kind, o in ((5, 3), (6, 1), (7, 2)):
            t_wait(q, kind, 2 * lax.rem(y + o, NY) + (1 - core))
        logits_chunk(q, tf, TW, Z, part, LOG2E / teacher_temp, None)

    t_far(0)

    @pl.loop(1, NCHUNK)
    def _(q):
        t_far(q)
        t_logits(q - 1)

    t_logits(NCHUNK - 1)

    sent = []

    def exchange(axis, buf, me, n, peer, send, recv):
        slot = buf.at[me]

        @pl.loop(0, n - 1)
        def _(i):
            remote(slot, slot, send, recv, **{axis: peer(i)}).start()

        region = buf.at[pl.ds(0, n - 1)]
        whole = remote(region, region, send, recv, **{axis: peer(0)})
        sent.append(whole)
        return whole.wait_recv

    def over_dp(i, buf):
        return exchange("dp", buf, j, NDP, dpeer, d_send.at[i], d_recv.at[i])

    def over_proto(i, buf):
        return exchange("proto", buf, p, NPR, ppeer, p_send.at[i], p_recv.at[i])

    def combine(buf, n, op):
        total = buf[0]
        for k in range(1, n):
            total = op(total, buf[k])
        return total

    def lane_reduce(part, reduce):
        rows = []
        for i in range(CBLK):
            rows.append(reduce(jnp.transpose(part[i * LANES:(i + 1) * LANES, :]), axis=0, keepdims=True))
        rows.append(jnp.zeros((8 - CBLK, LANES), F32))
        return jnp.concatenate(rows, axis=0)

    def to_columns(value, out):
        for i in range(CBLK):
            out[i * LANES:(i + 1) * LANES, :] = jnp.transpose(jnp.broadcast_to(value[i:i + 1, :], (LANES, LANES)))

    def exp_rows(first, last):
        @pl.loop(first // 8, last // 8)
        def _(r):
            rows = pl.ds(pl.multiple_of(r * 8, 8), 8)
            peak = zcol[rows, :]
            for g in range(GROUPS):
                lanes = pl.ds(g * LANES, LANES)
                Z[rows, lanes] = jnp.exp2(Z[rows, lanes] - peak)

    def proto_pass(out):
        for seg in range(NCHUNK):
            n = CHUNK // LANES

            def step(r, acc):
                rows = pl.ds(pl.multiple_of(r * 8, 8), 8)
                c = ccol[rows, :]
                return tuple(
                    acc[g] + Z[rows, pl.ds(seg * CHUNK + g * LANES, LANES)] * c for g in range(n)
                )

            acc = lax.fori_loop(0, CROPS // 8, step, tuple(jnp.zeros((8, LANES), F32) for _ in range(n)), unroll=8)
            for g in range(n):
                out[pl.ds(seg * n + g, 1), :] = jnp.sum(acc[g], axis=0, keepdims=True)

    def crop_pass():
        @pl.loop(0, CROPS // 32)
        def _(r):
            acc = [jnp.zeros((8, LANES), F32) for _ in range(4)]
            for g in range(GROUPS):
                scale = prow[:, g * LANES:(g + 1) * LANES]
                for k in range(4):
                    rows = pl.ds(pl.multiple_of(r * 32 + k * 8, 8), 8)
                    acc[k] = acc[k] + Z[rows, pl.ds(g * LANES, LANES)] * scale
            for k in range(4):
                part[pl.ds(pl.multiple_of(r * 32 + k * 8, 8), 8), :] = acc[k]

    def crop_loss_pass():
        @pl.loop(0, CROPS // 16)
        def _(r):
            acc = [jnp.zeros((8, LANES), F32) for _ in range(2)]
            acc2 = [jnp.zeros((8, LANES), F32) for _ in range(2)]
            rows = [pl.ds(pl.multiple_of(r * 16 + k * 8, 8), 8) for k in range(2)]
            lse = [lcol[rows[k], :] for k in range(2)]
            for g in range(GROUPS):
                scale = prow[:, g * LANES:(g + 1) * LANES]
                for k in range(2):
                    value = Z[rows[k], pl.ds(g * LANES, LANES)] * scale
                    acc[k] = acc[k] + value
                    acc2[k] = acc2[k] + value * (S[rows[k], pl.ds(g * LANES, LANES)] - lse[k])
            for k in range(2):
                part[rows[k], :] = acc[k]
                spart[rows[k], :] = acc2[k]

    def student_relay():
        for k, o in ((0, 3), (2, 1), (1, 2)):
            region = SW.at[rows_of(ypeer(o))]
            remote(region, region, s_send, s_recv.at[k], dp=sib).wait_recv()
            remote(region, region, s_send, s_recv.at[4 + k], dp=sib).start()

    def student_arrived():
        region = SW.at[rows_of(sib)]
        remote(region, region, s_send, s_recv.at[3], dp=sib).wait_recv()
        for k, o in ((0, 3), (2, 1), (1, 2)):
            region = SW.at[rows_of(2 * lax.rem(y + o, NY) + (1 - core))]
            remote(region, region, s_send, s_recv.at[4 + k], dp=sib).wait_recv()

    def student_chunk(q):
        logits_chunk(q, sf, SW, S, spart, LOG2E / student_temp, isn)

    def student_sums():
        peak = lane_reduce(spart, jnp.max)
        to_columns(peak, lcol)

        @pl.loop(0, CROPS // 8)
        def _(r):
            rows = pl.ds(pl.multiple_of(r * 8, 8), 8)
            top = lcol[rows, :]
            acc = [jnp.zeros((8, LANES), F32) for _ in range(4)]
            for g in range(GROUPS):
                acc[g % 4] = acc[g % 4] + jnp.exp2(S[rows, pl.ds(g * LANES, LANES)] - top)
            spart[rows, :] = (acc[0] + acc[1]) + (acc[2] + acc[3])
        return peak, lane_reduce(spart, jnp.sum)

    own_peak = lane_reduce(part, jnp.max)
    pbuf0[p] = own_peak
    wait = over_proto(0, pbuf0)
    to_columns(own_peak, zcol)
    exp_rows(0, CROPS)
    wait()
    peak = combine(pbuf0, NPR, jnp.maximum)
    adjust = jnp.exp2(own_peak - peak)
    to_columns(adjust, ccol)

    for it in range(ITERS):
        proto_pass(dbuf.at[it, j])
        wait = over_dp(it, dbuf.at[it])
        if it == 0:
            student_relay()
        if it == 1:
            student_chunk(NCHUNK - 1)
            s_peak, s_sum = student_sums()
            pbuf2[p, 8:16] = s_peak
            pbuf2[p, 16:24] = s_sum
        wait()
        pstmp[...] = 1.0 / (TOTAL_PROTOS * combine(dbuf.at[it], NDP, jnp.add))
        for g in range(GROUPS):
            prow[:, g * LANES:(g + 1) * LANES] = jnp.broadcast_to(pstmp[g:g + 1, :], (8, LANES))
        if it < 2:
            crop_pass()
        else:
            crop_loss_pass()
        crop_local = lane_reduce(part, jnp.sum) * adjust
        if it == 0:
            pbuf1[p] = crop_local
            wait = over_proto(1, pbuf1)
            student_arrived()
            for q in range(NCHUNK - 1):
                student_chunk(q)
            wait()
            crop_mass = combine(pbuf1, NPR, jnp.add)
        elif it == 1:
            pbuf2[p, 0:8] = crop_local
            over_proto(2, pbuf2)()
            crop_mass, top = pbuf2[0, 0:8], pbuf2[0, 8:16]
            for k in range(1, NPR):
                crop_mass = crop_mass + pbuf2[k, 0:8]
                top = jnp.maximum(top, pbuf2[k, 8:16])
            total = jnp.zeros((8, LANES), F32)
            for k in range(NPR):
                total = total + pbuf2[k, 16:24] * jnp.exp2(pbuf2[k, 8:16] - top)
            to_columns(top + jnp.log2(total), lcol)
        else:
            pbuf3[p, 0:8] = crop_local
            pbuf3[p, 8:16] = lane_reduce(spart, jnp.sum) * adjust
            over_proto(3, pbuf3)()
            both = combine(pbuf3, NPR, jnp.add)
            crop_mass = both[0:8]
        crop_scale = 1.0 / (TOTAL_CROPS * crop_mass)
        if it < 2:
            to_columns(crop_scale * adjust, ccol)
        else:
            to_columns(crop_scale * adjust * TOTAL_CROPS, ccol)
            crop_loss = (crop_scale * both[8:16])[0:CBLK]
            dbuf4[j, GROUPS:GROUPS + 8] = jnp.concatenate([crop_loss, jnp.zeros((8 - CBLK, LANES), F32)], axis=0)

    def fcols(f):
        return pl.ds(pl.multiple_of(f * FCHUNK, FCHUNK), FCHUNK)

    def sib_copy(f):
        return remote(sendsib.at[:, :, fcols(f)], recvsib.at[:, :, fcols(f)], sib_send, sib_recv.at[f], dp=sib)

    def via(f):
        return jnp.where(lax.rem(f, 2) == 0, right, left), jnp.where(lax.rem(f, 2) == 0, left, right)

    def y_copy(f, kind, to):
        return remote(
            sendy.at[kind, :, fcols(f)], recvy.at[kind, :, fcols(f)], y_send, y_recv.at[kind, f], dp=to
        )

    def chip_sum(index, f):
        slab = lax.div(index, 2)
        return ownf[slab, :, fcols(f)] + recvsib[slab, :, fcols(f)]

    def forward(f):
        sib_copy(f).wait_recv()
        near, away = via(f)
        sendy[0, :, fcols(f)] = chip_sum(far, f).astype(BF16)
        y_copy(f, 0, near).start()
        sendy[1, :, fcols(f)] = chip_sum(away, f).astype(BF16)
        y_copy(f, 1, away).start()

    def forward_direct(f):
        sib_copy(f).wait_recv()
        near, away = via(f)
        for kind, to in ((0, far), (1, away), (2, near)):
            sendy[kind, :, fcols(f)] = chip_sum(to, f).astype(BF16)
            y_copy(f, kind, to).start()

    def pass_on(f):
        near, away = via(f)
        y_copy(f, 0, near).wait_recv()
        sendy[2, :, fcols(f)] = (chip_sum(near, f) + recvy[0, :, fcols(f)].astype(F32)).astype(BF16)
        y_copy(f, 2, near).start()

    @pl.loop(0, NF)
    def _(f):
        scale = jnp.broadcast_to(prow[0:1, fcols(f)], (16, FCHUNK))
        n = FCHUNK // LANES

        def step(r, pressure):
            rows = pl.ds(pl.multiple_of(r * 16, 16), 16)
            c = jnp.concatenate([ccol[rows, :]] * n, axis=1)
            l = jnp.concatenate([lcol[rows, :]] * n, axis=1)
            assign = Z[rows, fcols(f)] * scale * c
            codes[rows, fcols(f)] = assign.astype(BF16)
            s = S[rows, fcols(f)]
            logp = s - l
            signal = ((jnp.exp2(logp) - assign) * (1.0 / student_temp)).astype(BF16)
            sig[rows, :] = signal
            return pressure + signal.astype(F32) * s

        pressure = lax.fori_loop(0, CROPS // 16, step, jnp.zeros((16, FCHUNK), F32), unroll=4)
        pressure = jnp.sum(pressure, axis=0, keepdims=True) * (LN2 * student_temp)
        for g in range(n):
            dbuf4[j, pl.ds(f * n + g, 1), :] = pressure[:, g * LANES:(g + 1) * LANES]
        other = jnp.dot(sfT[1 - core], sig[...], preferred_element_type=F32)
        sendsib[:, :, fcols(f)] = other.reshape(NY, SLAB, FCHUNK)
        sib_copy(f).start()
        own = jnp.dot(sfT[core], sig[...], preferred_element_type=F32)
        ownf[:, :, fcols(f)] = own.reshape(NY, SLAB, FCHUNK)

        @pl.when(f >= 2)
        def _():
            forward(f - 2)

        @pl.when(f >= 4)
        def _():
            pass_on(f - 4)

    wait = over_dp(3, dbuf4)
    forward_direct(NF - 2)
    pass_on(NF - 4)
    forward_direct(NF - 1)
    pass_on(NF - 3)
    wait()
    total = combine(dbuf4, NDP, jnp.add)
    pstmp[...] = total[:GROUPS]
    loss_out[0, 0] = jnp.sum(total[GROUPS:]) * (-LN2)

    for f in range(NF):
        cols = slice(f * FCHUNK, (f + 1) * FCHUNK)
        y_copy(f, 1, left).wait_recv()
        y_copy(f, 2, left).wait_recv()
        pressure = jnp.concatenate(
            [pstmp[f * 4 + g:f * 4 + g + 1, :] for g in range(FCHUNK // LANES)], axis=1
        )
        inverse = isn[0:1, cols]
        direct = ownf[y, :, cols] + recvsib[y, :, cols]
        direct = direct + (recvy[1, :, cols].astype(F32) + recvy[2, :, cols].astype(F32))
        if f >= NF - 2:
            y_copy(f, 0, left).wait_recv()
            direct = direct + recvy[0, :, cols].astype(F32)
        weight = sw_rows(SW, j, cols).astype(F32)
        grad[:, cols] = (direct - weight * (inverse * pressure)) * inverse

    for whole in sent:
        whole.wait_send()
    region = TW.at[pl.ds(0, 7 * SLAB)]
    remote(region, region, t_send, t_recv.at[0, 0], dp=sib).wait_send()
    region = SW.at[pl.ds(0, 7 * SLAB)]
    remote(region, region, s_send, s_recv.at[0], dp=sib).wait_send()
    remote(sendsib, recvsib, sib_send, sib_recv.at[0], dp=sib).wait_send()
    remote(sendy, recvy, y_send, y_recv.at[0, 0], dp=right).wait_send()


def write_kernel(codes, grad, codes_out, grad_out, code_sem, grad_sem):
    rows = CROPS // NWRITE
    copies = [pltpu.make_async_copy(grad, grad_out, grad_sem)]
    for i in range(NWRITE):
        part = pl.ds(i * rows, rows)
        copies.append(pltpu.make_async_copy(codes.at[part], codes_out.at[part], code_sem.at[i]))
    for copy in copies:
        copy.start()
    for copy in copies:
        copy.wait()


def sw_rows(SW, j, cols):
    return SW[pl.ds(pl.multiple_of(j * SLAB, 16), SLAB), cols]


def body(teacher_features, student_features, teacher_weight, student_weight):
    vmem = pl.BlockSpec(memory_space=pltpu.VMEM)
    hbm = pl.BlockSpec(memory_space=pl.ANY)
    dma = pltpu.SemaphoreType.DMA
    codes, loss, grad = pl.pallas_call(
        head_kernel,
        out_shape=(
            pltpu.VMEM((CROPS, PROTOS), BF16),
            jax.ShapeDtypeStruct((1, 1), F32),
            pltpu.VMEM((SLAB, PROTOS), F32),
        ),
        in_specs=[vmem, vmem, hbm, hbm],
        out_specs=(vmem, pl.BlockSpec(memory_space=pltpu.SMEM), vmem),
        scratch_shapes=[
            pltpu.VMEM((BOTTLE, PROTOS), BF16),
            pltpu.VMEM((BOTTLE, PROTOS), BF16),
            pltpu.VMEM((CROPS, PROTOS), F32),
            pltpu.VMEM((CROPS, PROTOS), F32),
            pltpu.VMEM((2, BOTTLE // 2, CROPS), BF16),
            pltpu.VMEM((CROPS, LANES), F32),
            pltpu.VMEM((CROPS, LANES), F32),
            pltpu.VMEM((CROPS, LANES), F32),
            pltpu.VMEM((CROPS, LANES), F32),
            pltpu.VMEM((CROPS, LANES), F32),
            pltpu.VMEM((8, CHUNK), F32),
            pltpu.VMEM((8, PROTOS), F32),
            pltpu.VMEM((GROUPS, LANES), F32),
            pltpu.VMEM((8, PROTOS), F32),
            pltpu.VMEM((CROPS, FCHUNK), BF16),
            pltpu.VMEM((NY, SLAB, PROTOS), F32),
            pltpu.VMEM((NY, SLAB, PROTOS), F32),
            pltpu.VMEM((NY, SLAB, PROTOS), F32),
            pltpu.VMEM((NY - 1, SLAB, PROTOS), BF16),
            pltpu.VMEM((NY - 1, SLAB, PROTOS), BF16),
            pltpu.VMEM((ITERS, NDP, GROUPS, LANES), F32),
            pltpu.VMEM((NDP, GROUPS + 8, LANES), F32),
            pltpu.VMEM((NPR, 8, LANES), F32),
            pltpu.VMEM((NPR, 8, LANES), F32),
            pltpu.VMEM((NPR, 24, LANES), F32),
            pltpu.VMEM((NPR, 16, LANES), F32),
            dma((2,)), dma, dma((NCHUNK, 8)), dma, dma((7,)),
            dma((4,)), dma((4,)), dma((4,)), dma((4,)),
            dma, dma((NF,)), dma, dma((NY - 1, NF)),
        ],
        compiler_params=pltpu.CompilerParams(
            collective_id=0, has_side_effects=True, vmem_limit_bytes=54 * 1024 * 1024
        ),
    )(teacher_features, student_features, teacher_weight, student_weight)
    codes, grad = pl.pallas_call(
        write_kernel,
        out_shape=(
            jax.ShapeDtypeStruct((CROPS, PROTOS), BF16),
            jax.ShapeDtypeStruct((SLAB, PROTOS), F32),
        ),
        in_specs=[vmem, vmem],
        out_specs=(hbm, hbm),
        scratch_shapes=[dma((NWRITE,)), dma],
        compiler_params=pltpu.CompilerParams(vmem_limit_bytes=1024 * 1024),
    )(codes, grad)
    return codes, loss[0, 0], grad


def solution(mesh):
    return jax.shard_map(
        body,
        mesh=mesh,
        in_specs=(P("dp", None), P("dp", None), P("dp", "proto"), P("dp", "proto")),
        out_specs=(P("dp", "proto"), P(), P("dp", "proto")),
        check_vma=False,
    )
```
